32 devices in a mesh: ctx: 8 (over z, x), head: 4 (over y, core).
Axes of the slice: x: 2, y: 2, z: 4, core: 2. Of those that a mesh axis runs over, the one named last changes fastest.
Arguments:
- query: bfloat16 [8192, 4096], P(('ctx', 'head')), may hold values from -90 to 90
- keys: bfloat16 [8192, 4096], P(('ctx', 'head')), may hold values from -4.5 to 4.5
- values: bfloat16 [8192, 4096], P(('ctx', 'head')), may hold values from -5 to 5
- grad_out: bfloat16 [8192, 4096], P(('ctx', 'head')), may hold values from -5 to 5
- random_owner: int32 [64, 3], replicated, may hold values from 0 to 7, all different within a row; in each aligned block of 8 rows (0 to 7, 8 to 15, ...) at most 4 rows name the same one
- random_within: int32 [64, 3], replicated, may hold values from 0 to 7
- global_ids: int32 [64, 2], replicated, may hold values from 0 to 3, all different within a row
Outputs:
- grad_query: bfloat16 [8192, 4096], P(('ctx', 'head'))
- grad_keys: bfloat16 [8192, 4096], P(('ctx', 'head'))
- grad_values: bfloat16 [8192, 4096], P(('ctx', 'head'))
The draws below stay inside these ranges and needn't reach their ends.
Inputs may be any that keep to these rules, and one draw needn't show every extreme that they name: `random_owner`: in the 8 rows of one index of ctx no owner is named more than 4 times, a bound that some block reaches in some of them; the 3 owners of one row differ. `global_ids`: the 2 blocks of one row differ; every block 0 to 3 is named by some row.
All inputs are finite; a program needn't handle non-finite values.
Results may differ from the reference program's by a relative error of at most 0.0053.
Values may be sent and summed in bfloat16 or wider, within the bound.
A program may use at most 320 MiB of HBM per device.

```python
import math
import jax
import jax.numpy as jnp
import numpy as np
from jax import lax

HEADS = 32
HEAD_DIM = 128
BLOCK = 128
BPD = 8
RAND = 3
GLOB = 2
NGLOB = 4
CAP = 4
QBLOCKS = 64
SEQ = 8192
N_CTX = 8


def draw_pair(key):
    base_key = jax.random.fold_in(key, 11)
    key_keys, key_query = jax.random.split(base_key, 2)
    full_shape = (SEQ, HEADS * HEAD_DIM)
    keys_draw = jnp.clip(jax.random.normal(key_keys, full_shape, jnp.float32), -4.5, 4.5)
    query_draw = jnp.clip(jax.random.normal(key_query, full_shape, jnp.float32), -4.5, 4.5)
    return (query_draw, keys_draw)


def draw_query(key, part):
    return draw_pair(key)[0].astype(jnp.bfloat16)


def draw_keys(key, part):
    return draw_pair(key)[1].astype(jnp.bfloat16)


def touch_ends(drawn, key, low, high):
    longest = drawn.shape.index(max(drawn.shape))
    spots = []
    for shift in (0, 1):
        where = [jax.random.randint(jax.random.fold_in(key, axis), (), 0, length) for axis, length in enumerate(drawn.shape)]
        where[longest] = (where[longest] + shift) % drawn.shape[longest]
        spots.append(tuple(where))
    return drawn.at[spots[0]].set(low).at[spots[1]].set(high)


def steps_of(own_key, extent, pieces, least, top_value):
    def one(dim, blocks):
        heights = jax.random.uniform(jax.random.fold_in(jax.random.fold_in(own_key, 6), dim), (blocks,), jnp.float32, least / len(pieces), top_value / len(pieces))
        return jnp.repeat(jnp.exp(heights), extent[dim] // blocks).reshape((-1,) + (1,) * (len(extent) - dim - 1))

    level = one(*pieces[0])
    for cut in pieces[1:]:
        level = level * one(*cut)
    return level


def choose_distinct(stream_key, rows, count, top, lift):
    order = jax.random.permutation(jax.random.fold_in(stream_key, 1), count)
    favour = order
    for power in range(3):
        favour = favour * favour // count
    favour = favour * lift // count
    lots = jax.random.randint(jax.random.fold_in(stream_key, 2), (rows, count), 0, 4096) + favour
    fixed_rows = jax.random.permutation(jax.random.fold_in(stream_key, 3), rows)[jnp.arange(count) % rows]
    lots = jnp.where(jnp.arange(rows)[:, None] == fixed_rows[None, :], 1 << 14, lots)
    priority = lots * count + jnp.arange(count)
    return lax.top_k(priority.astype(jnp.int32), top)[1].astype(jnp.int32)


def deal_out(stream_key, own, number, rows, count, top, most, slope):
    sequence = jax.random.permutation(stream_key, count)
    crowded, usual = shares(count, rows * top, most, slope, True), shares(count, rows * top, most, slope, False)
    places = jnp.arange(count)

    def named(tallies, offset_by):
        used = int((tallies > 0).sum())
        fixed = max(1, used // 4)
        moved = fixed + (places - fixed + offset_by * (used - fixed)) % max(1, count - fixed)
        return jnp.zeros((count,), jnp.int32).at[sequence[jnp.where(places < fixed, places, moved)]].set(jnp.asarray(tallies, jnp.int32))

    tallies = jnp.where(number % 4 == 0, named(crowded, number // 4), named(usual, number - number // 4 - 1))
    mixed = jax.random.permutation(jax.random.fold_in(own, 3), count)
    giver, sink = mixed[0:count // 2 * 2:2], mixed[1:count // 2 * 2:2]
    margin = jnp.minimum(tallies[giver] - 1, most - tallies[sink]) // 2
    margin = jnp.where((giver == sequence[0]) | (sink == sequence[0]) | (tallies[sink] == 0), 0, jnp.maximum(margin, 0))
    moved = jax.random.randint(jax.random.fold_in(own, 4), (count // 2,), 0, 1 << 20) % (margin + 1)
    tallies = tallies.at[giver].add(-moved).at[sink].add(moved)
    items = jnp.searchsorted(jnp.cumsum(tallies), jnp.arange(rows * top), side="right").astype(jnp.int32)
    table = items.reshape(top, rows).T
    table = table[jax.random.permutation(jax.random.fold_in(own, 1), rows)]
    offset_by = jax.random.randint(jax.random.fold_in(own, 2), (rows, 1), 0, top)
    return jnp.take_along_axis(table, (jnp.arange(top)[None, :] + offset_by) % top, axis=1)


def shares(amount, total, most, slope, full):
    loads = [(1 << 20) // math.isqrt(grade ** slope) + 1 for grade in range(1, amount + 1)]
    largest = most if full else min(most, max(-(-total // amount), total * loads[0] // sum(loads)))
    least = 1 if total - largest >= amount - 1 else 0
    given, spare = [largest] + [least] * (amount - 1), total - largest - least * (amount - 1)
    while spare > 0:
        movable = [i for i in range(1, amount) if given[i] < largest] or [i for i in range(1, amount) if given[i] < most]
        mass, left = sum([loads[i] for i in movable]), spare
        for i in movable:
            more = min(most - given[i], max(1, left * loads[i] // mass), spare)
            given[i] = given[i] + more
            spare = spare - more
    return np.array(given)


def scatter_about(rng, extent, deviation, most, cuts=(), held_as=jnp.bfloat16):
    entries = jax.random.normal(rng, extent, jnp.float32) * deviation
    if len(cuts) > 0:
        entries = steps_of(rng, extent, cuts, -0.22, 0.18) * entries
    return jnp.clip(entries, min=-most, max=most).astype(held_as)


def setup_inputs(seed: int = 0) -> dict:
    streams_of = jax.random.split(jax.random.key(seed), 8)
    query = draw_query(jax.random.fold_in(streams_of[7], 71), 0)
    keys = draw_keys(jax.random.fold_in(streams_of[7], 71), 0)
    values = scatter_about(streams_of[2], (SEQ, HEADS * HEAD_DIM), 1.0, 5.0, ((0, 32),))
    grad_out = scatter_about(streams_of[3], (SEQ, HEADS * HEAD_DIM), 1.0, 5.0, ((0, 32),))
    random_owner_keys = jax.random.split(jax.random.fold_in(streams_of[4], 1), QBLOCKS // BPD)
    random_owner_turns = jax.random.permutation(jax.random.fold_in(streams_of[4], 3), QBLOCKS // BPD)
    random_owner = jax.vmap(lambda own, number: deal_out(jax.random.fold_in(streams_of[4], 2), own, number, BPD, N_CTX, RAND, CAP, 2))(random_owner_keys, random_owner_turns).reshape((QBLOCKS, RAND))
    random_within = touch_ends(jax.random.randint(streams_of[5], (QBLOCKS, RAND), 0, BPD), jax.random.fold_in(streams_of[5], 1), 0, BPD - 1).astype(jnp.int32)
    global_ids = choose_distinct(streams_of[6], QBLOCKS, NGLOB, GLOB, 4096)
    return {"query": query, "keys": keys, "values": values, "grad_out": grad_out, "random_owner": random_owner, "random_within": random_within, "global_ids": global_ids}


def reference(query, keys, values, grad_out, random_owner, random_within, global_ids):
    blocks = SEQ // BLOCK
    score_scale = HEAD_DIM ** -0.5
    block_shape = (blocks, BLOCK, HEADS, HEAD_DIM)
    query_blocks = query.reshape(block_shape)
    key_blocks = keys.reshape(block_shape)
    value_blocks = values.reshape(block_shape)
    grad_blocks = grad_out.reshape(block_shape)
    indices = jnp.arange(blocks, dtype=jnp.int32)
    random_ids = (random_owner * BPD + random_within).astype(jnp.int32)
    key_lists = jnp.concatenate([(indices - 1)[:, None], indices[:, None], (indices + 1)[:, None], global_ids.astype(jnp.int32), random_ids], axis=1)
    list_valid = (key_lists >= 0) & (key_lists < blocks)
    safe_lists = jnp.clip(key_lists, 0, blocks - 1).astype(jnp.int32)
    slot_random = jnp.arange(3 + GLOB + RAND) >= 3 + GLOB

    def one_block(carried, index):
        sum_keys, sum_values = carried
        key_ids = safe_lists[index]
        slot_ok = list_valid[index]
        query_f = query_blocks[index].astype(jnp.float32)
        grad_f = grad_blocks[index].astype(jnp.float32)
        keys_f = key_blocks[key_ids].astype(jnp.float32)
        values_f = value_blocks[key_ids].astype(jnp.float32)
        scores = jnp.einsum("qhd,nkhd->hqnk", query_f, keys_f) * score_scale
        scores = jnp.where(slot_ok[None, None, :, None], scores, -jnp.inf)
        highest = jnp.max(scores, axis=(2, 3), keepdims=True)
        logsum = highest + jnp.log(jnp.sum(jnp.exp(scores - highest), axis=(2, 3), keepdims=True))
        probs = jnp.exp(scores - logsum)
        probs_low = lax.optimization_barrier(probs.astype(jnp.bfloat16)).astype(jnp.float32)
        dprobs = jnp.einsum("qhd,nkhd->hqnk", grad_f, values_f)
        row_dot = jnp.sum(probs * dprobs, axis=(2, 3), keepdims=True)
        dscores = lax.optimization_barrier((probs * (dprobs - row_dot)).astype(jnp.bfloat16)).astype(jnp.float32)
        grad_query = jnp.einsum("hqnk,nkhd->qhd", dscores, keys_f) * score_scale
        key_terms = jnp.einsum("hqnk,qhd->nkhd", dscores, query_f) * score_scale
        value_terms = jnp.einsum("hqnk,qhd->nkhd", probs_low, grad_f)
        key_rounded = lax.optimization_barrier(key_terms.astype(jnp.bfloat16)).astype(jnp.float32)
        value_rounded = lax.optimization_barrier(value_terms.astype(jnp.bfloat16)).astype(jnp.float32)
        key_terms = jnp.where(slot_random[:, None, None, None], key_rounded, key_terms)
        value_terms = jnp.where(slot_random[:, None, None, None], value_rounded, value_terms)
        sum_keys = sum_keys.at[key_ids].add(key_terms)
        sum_values = sum_values.at[key_ids].add(value_terms)
        return (sum_keys, sum_values), grad_query.astype(jnp.bfloat16)

    zero_sums = jnp.zeros(block_shape, jnp.float32)
    finals, grad_queries = lax.scan(one_block, (zero_sums, zero_sums), indices)
    grad_query = grad_queries.reshape(SEQ, HEADS * HEAD_DIM)
    grad_keys = finals[0].reshape(SEQ, HEADS * HEAD_DIM).astype(jnp.bfloat16)
    grad_values = finals[1].reshape(SEQ, HEADS * HEAD_DIM).astype(jnp.bfloat16)
    return (grad_query, grad_keys, grad_values)
```

```python
from functools import partial

import jax
import jax.numpy as jnp
from jax import lax
from jax.experimental import pallas as pl
from jax.experimental.pallas import tpu as pltpu
from jax.sharding import PartitionSpec as P


HEAD_DIM = 128
BLOCK = 128
RAND = 3
GLOB = 2
NGLOB = 4
SLOTS = 3 + GLOB + RAND
CHUNKS = 2
SCALE = HEAD_DIM ** (-0.5)
LOG2E = 1.4426950408889634
NEG = -1e30
VMEM_LIMIT = 60 * 1024 * 1024


def dot(a, b, dims):
    return lax.dot_general(a, b, (dims, ((), ())), preferred_element_type=jnp.float32)


def pack_kernel(own_idx, far_idx, *refs, groups):
    outs = refs[-groups:]
    for m in range(groups):
        outs[m][0, 0] = refs[2 * m][...]
        outs[m][1, 0] = refs[2 * m + 1][...]


def pack(own_idx, far_idx, kv, kv_far, ready, groups, cap):
    features = kv.shape[-1]
    block = (2, BLOCK, features)
    in_specs, args = [], []
    for m in range(groups):
        in_specs.append(pl.BlockSpec(block, lambda c, oi, fi, m=m: (0, oi[m * cap + c], 0)))
        in_specs.append(pl.BlockSpec(block, lambda c, oi, fi, m=m: (0, fi[m * cap + c], 0)))
        args += [kv, kv_far]
    in_specs += [pl.BlockSpec(memory_space=pl.ANY)] * len(ready)
    return pl.pallas_call(
        partial(pack_kernel, groups=groups),
        grid_spec=pltpu.PrefetchScalarGridSpec(
            num_scalar_prefetch=2,
            grid=(cap,),
            in_specs=in_specs,
            out_specs=[
                pl.BlockSpec((2, 1, 2, BLOCK, features), lambda c, *_: (0, c, 0, 0, 0))
            ] * groups,
        ),
        out_shape=[jax.ShapeDtypeStruct((2, cap, 2, BLOCK, features), kv.dtype)] * groups,
        compiler_params=pltpu.CompilerParams(vmem_limit_bytes=VMEM_LIMIT),
        name="pack",
    )(own_idx, far_idx, *args, *ready)


def attn_kernel(
    gid_ref,
    slot_ref,
    edge_ref,
    q_ref,
    g_ref,
    kv_ref,
    left_ref,
    right_ref,
    sum_ref,
    *refs,
    blocks,
    groups,
    each,
):
    incs, refs = refs[:groups], refs[groups:]
    dq_ref, own_ref, dleft_ref, dright_ref, dsum_ref = refs[:5]
    term_outs = refs[5 : 5 + groups]
    kwin, vwin, kcat, vcat, dkw, dvw, sacc, inc_ref, terms_ref = refs[5 + groups :]
    for m in range(groups):
        inc_ref[m * each : (m + 1) * each] = incs[m][...]
    rows = blocks * BLOCK
    for win, x in ((kwin, 0), (vwin, 1)):
        win[0:BLOCK] = left_ref[x]
        win[BLOCK : BLOCK + rows] = kv_ref[x]
        win[BLOCK + rows :] = right_ref[x]
    dkw[...] = jnp.zeros_like(dkw)
    dvw[...] = jnp.zeros_like(dvw)
    sacc[...] = jnp.zeros_like(sacc)
    terms_ref[...] = jnp.zeros_like(terms_ref)

    def step(i, carry):
        base = pl.multiple_of(i * BLOCK, BLOCK)
        here = pl.ds(base, BLOCK)
        window = pl.ds(base, 3 * BLOCK)
        kcat[0 : 3 * BLOCK] = kwin[window]
        vcat[0 : 3 * BLOCK] = vwin[window]
        for n in range(GLOB):
            gid = pl.multiple_of(gid_ref[i * GLOB + n] * BLOCK, BLOCK)
            at = slice((3 + n) * BLOCK, (4 + n) * BLOCK)
            kcat[at] = sum_ref[0, pl.ds(gid, BLOCK)]
            vcat[at] = sum_ref[1, pl.ds(gid, BLOCK)]
        for n in range(RAND):
            slot = slot_ref[i * RAND + n]
            at = slice((3 + GLOB + n) * BLOCK, (4 + GLOB + n) * BLOCK)
            kcat[at] = inc_ref[slot, 0]
            vcat[at] = inc_ref[slot, 1]
        q = q_ref[here]
        g = g_ref[here]
        keys = kcat[...]
        s = dot(keys, q, ((1,), (1,)))
        no_left = (i == 0) & (edge_ref[0] == 1)
        no_right = (i == blocks - 1) & (edge_ref[1] == 1)
        s = jnp.concatenate(
            [
                jnp.where(no_left, NEG, s[0:BLOCK]),
                s[BLOCK : 2 * BLOCK],
                jnp.where(no_right, NEG, s[2 * BLOCK : 3 * BLOCK]),
                s[3 * BLOCK :],
            ],
            axis=0,
        )
        highest = jnp.max(s, axis=0, keepdims=True)
        e = jnp.exp2((s - highest) * (SCALE * LOG2E))
        p = e * (1.0 / jnp.sum(e, axis=0, keepdims=True))
        dp = dot(vcat[...], g, ((1,), (1,)))
        row_dot = jnp.sum(p * dp, axis=0, keepdims=True)
        ds = (p * (dp - row_dot)).astype(jnp.bfloat16)
        p_low = p.astype(jnp.bfloat16)
        dq = dot(ds, keys, ((0,), (0,))) * SCALE
        dq_ref[here] = dq.astype(jnp.bfloat16)
        dk = dot(ds, q, ((1,), (0,))) * SCALE
        dv = dot(p_low, g, ((1,), (0,)))
        dkw[window] += dk[0 : 3 * BLOCK]
        dvw[window] += dv[0 : 3 * BLOCK]
        for n in range(GLOB):
            gid = pl.multiple_of(gid_ref[i * GLOB + n] * BLOCK, BLOCK)
            at = slice((3 + n) * BLOCK, (4 + n) * BLOCK)
            sacc[0, pl.ds(gid, BLOCK)] += dk[at]
            sacc[1, pl.ds(gid, BLOCK)] += dv[at]
        for n in range(RAND):
            slot = slot_ref[i * RAND + n]
            at = slice((3 + GLOB + n) * BLOCK, (4 + GLOB + n) * BLOCK)
            terms_ref[slot, 0] = dk[at].astype(jnp.bfloat16)
            terms_ref[slot, 1] = dv[at].astype(jnp.bfloat16)
        return carry

    lax.fori_loop(0, blocks, step, 0)
    for acc, x in ((dkw, 0), (dvw, 1)):
        dleft_ref[x] = acc[0:BLOCK].astype(jnp.bfloat16)
        own_ref[x] = acc[BLOCK : BLOCK + rows]
        dright_ref[x] = acc[BLOCK + rows :].astype(jnp.bfloat16)
    dsum_ref[...] = sacc[...].astype(jnp.bfloat16)
    for m in range(groups):
        term_outs[m][...] = terms_ref[m * each : (m + 1) * each]


def attention(gids, slots, edges, q, g, kv, left, right, summary, incoming):
    rows, features = q.shape
    blocks = rows // BLOCK
    groups = len(incoming)
    each = incoming[0].shape[0]
    col = lambda h, *_: (0, h)
    col3 = lambda h, *_: (0, 0, h)
    col4 = lambda h, *_: (0, 0, 0, h)
    tok = pl.BlockSpec((rows, HEAD_DIM), col)
    halo = pl.BlockSpec((2, BLOCK, HEAD_DIM), col3)
    summ = pl.BlockSpec((2, NGLOB * BLOCK, HEAD_DIM), col3)
    inc = pl.BlockSpec((each, 2, BLOCK, HEAD_DIM), col4)
    pair = pl.BlockSpec((2, rows, HEAD_DIM), col3)
    low = jnp.bfloat16
    wide = rows + 2 * BLOCK
    return pl.pallas_call(
        partial(attn_kernel, blocks=blocks, groups=groups, each=each),
        grid_spec=pltpu.PrefetchScalarGridSpec(
            num_scalar_prefetch=3,
            grid=(features // HEAD_DIM,),
            in_specs=[tok, tok, pair, halo, halo, summ] + [inc] * groups,
            out_specs=[
                tok,
                pair,
                halo,
                halo,
                summ,
            ]
            + [inc] * groups,
            scratch_shapes=[
                pltpu.VMEM((wide, HEAD_DIM), low),
                pltpu.VMEM((wide, HEAD_DIM), low),
                pltpu.VMEM((SLOTS * BLOCK, HEAD_DIM), low),
                pltpu.VMEM((SLOTS * BLOCK, HEAD_DIM), low),
                pltpu.VMEM((wide, HEAD_DIM), jnp.float32),
                pltpu.VMEM((wide, HEAD_DIM), jnp.float32),
                pltpu.VMEM((2, NGLOB * BLOCK, HEAD_DIM), jnp.float32),
                pltpu.VMEM((groups * each, 2, BLOCK, HEAD_DIM), low),
                pltpu.VMEM((groups * each, 2, BLOCK, HEAD_DIM), low),
            ],
        ),
        out_shape=[
            jax.ShapeDtypeStruct((rows, features), low),
            jax.ShapeDtypeStruct((2, rows, features), jnp.float32),
            jax.ShapeDtypeStruct((2, BLOCK, features), low),
            jax.ShapeDtypeStruct((2, BLOCK, features), low),
            jax.ShapeDtypeStruct((2, NGLOB * BLOCK, features), low),
        ]
        + [jax.ShapeDtypeStruct((each, 2, BLOCK, features), low)] * groups,
        compiler_params=pltpu.CompilerParams(vmem_limit_bytes=VMEM_LIMIT),
        name="attention",
    )(gids, slots, edges, q, g, kv, left, right, summary, *incoming)


def add_slots(acc, idx_ref, incs, cap):
    for m, inc in enumerate(incs):
        for c in range(cap):
            at = pl.ds(pl.multiple_of(idx_ref[m * cap + c] * BLOCK, BLOCK), BLOCK)
            acc[0, at] += inc[0, c, 0].astype(jnp.float32)
            acc[1, at] += inc[0, c, 1].astype(jnp.float32)


def far_kernel(idx_ref, *refs, groups, cap):
    sum_refs = refs[groups : 2 * groups]
    out_ref, total_ref, acc = refs[2 * groups :]
    acc[...] = jnp.zeros_like(acc)
    total = sum_refs[0][...].astype(jnp.float32)
    for ref in sum_refs[1:]:
        total += ref[...].astype(jnp.float32)
    total_ref[...] = total

    @pl.when(idx_ref[groups * cap] == 1)
    def _():
        acc[:, 0 : NGLOB * BLOCK] += total

    add_slots(acc, idx_ref, refs[:groups], cap)
    out_ref[...] = acc[...].astype(jnp.bfloat16)


def own_kernel(idx_ref, *refs, groups, cap):
    own_ref, far_ref, first_ref, last_ref, sum_ref, dk_ref, dv_ref, acc = refs[groups:]
    rows = own_ref.shape[1]
    acc[...] = own_ref[...] + far_ref[...].astype(jnp.float32)
    acc[:, 0:BLOCK] += first_ref[...].astype(jnp.float32)
    acc[:, rows - BLOCK :] += last_ref[...].astype(jnp.float32)

    @pl.when(idx_ref[groups * cap] == 1)
    def _():
        acc[:, 0 : NGLOB * BLOCK] += sum_ref[...]

    add_slots(acc, idx_ref, refs[:groups], cap)
    dk_ref[...] = acc[0].astype(jnp.bfloat16)
    dv_ref[...] = acc[1].astype(jnp.bfloat16)


def combine(kernel, side, idx, incoming, extra, rows, out_specs, out_shape):
    groups = len(incoming)
    cap = incoming[0].shape[1]
    features = incoming[0].shape[-1]
    col3 = lambda h, *_: (0, 0, h)
    spec3 = lambda x: pl.BlockSpec(x.shape[:2] + (HEAD_DIM,), col3)
    inc = pl.BlockSpec((1, cap, 2, BLOCK, HEAD_DIM), lambda h, *_: (side, 0, 0, 0, h))
    return pl.pallas_call(
        partial(kernel, groups=groups, cap=cap),
        grid_spec=pltpu.PrefetchScalarGridSpec(
            num_scalar_prefetch=1,
            grid=(features // HEAD_DIM,),
            in_specs=[inc] * groups + [spec3(x) for x in extra],
            out_specs=out_specs,
            scratch_shapes=[pltpu.VMEM((2, rows, HEAD_DIM), jnp.float32)],
        ),
        out_shape=out_shape,
        compiler_params=pltpu.CompilerParams(vmem_limit_bytes=VMEM_LIMIT),
    )(idx, *incoming, *extra)


def head_kernel(
    tab_ref,
    wt_ref,
    k_in,
    v_in,
    q_in,
    g_in,
    dq_out,
    dk_out,
    dv_out,
    kb,
    vb,
    qb,
    gb,
    dqb,
    dkb,
    dvb,
    dka,
    dva,
    terms_k,
    terms_v,
    run,
    kcat,
    vcat,
    in_send,
    in_recv,
    out_send,
    out_recv,
):
    heads = lax.axis_size("head")
    count = lax.axis_size("ctx") * heads
    half = count // 2
    me = lax.axis_index("ctx") * heads + lax.axis_index("head")
    mine = lax.div(me, half)
    each = k_in.shape[0]
    blocks = count * each
    entries = blocks * RAND
    at_gid, at_rid = 0, blocks * GLOB
    at_perm = at_rid + entries
    at_last = at_perm + entries
    at_carry = blocks * GLOB * NGLOB
    at_has = at_carry + entries

    def side(o):
        return lax.rem(mine + 1 + lax.div(o, half), 2) * half

    def target(o):
        return side(o) + lax.rem(me + lax.rem(o, half), half)

    def source(o):
        return side(o) + lax.rem(me + half - lax.rem(o, half), half)

    def coords(t):
        return (lax.div(t, heads), lax.rem(t, heads))

    def rows_of(s):
        return pl.ds(s * each, each)

    def rows_padded(s):
        return pl.ds(s * each + 1, each)

    def cols_of(s):
        return pl.ds(pl.multiple_of(s * HEAD_DIM, HEAD_DIM), HEAD_DIM)

    ins = ((k_in, kb, rows_padded), (v_in, vb, rows_padded), (q_in, qb, rows_of), (g_in, gb, rows_of))
    outs = ((dqb, dq_out), (dvb, dv_out), (dkb, dk_out))

    def bring(a, t, s):
        x, y, rows = ins[a]
        return pltpu.make_async_remote_copy(
            src_ref=x.at[:, :, cols_of(t)],
            dst_ref=y.at[rows(s)],
            send_sem=in_send.at[a, t],
            recv_sem=in_recv.at[a, s],
            device_id=coords(t),
            device_id_type=pl.DeviceIdType.MESH,
        )

    def bring_own(a):
        x, y, rows = ins[a]
        return pltpu.make_async_copy(x.at[:, :, cols_of(me)], y.at[rows(me)], in_recv.at[a, me])

    def give(a, t, s):
        x, y = outs[a]
        return pltpu.make_async_remote_copy(
            src_ref=x.at[rows_of(t)],
            dst_ref=y.at[:, :, cols_of(s)],
            send_sem=out_send.at[a, t],
            recv_sem=out_recv.at[a, s],
            device_id=coords(t),
            device_id_type=pl.DeviceIdType.MESH,
        )

    def give_own(a):
        x, y = outs[a]
        return pltpu.make_async_copy(x.at[rows_of(me)], y.at[:, :, cols_of(me)], out_recv.at[a, me])

    def peers(body):
        def run_body(o, carry):
            body(o)
            return carry

        lax.fori_loop(0, half, run_body, 0)
        lax.fori_loop(half + 1, count, run_body, 0)

    barrier = pltpu.get_barrier_semaphore()
    peers(
        lambda o: pl.semaphore_signal(
            barrier, inc=1, device_id=coords(target(o)), device_id_type=pl.DeviceIdType.MESH
        )
    )
    pl.semaphore_wait(barrier, count - 1)

    for pair in ((0, 1), (2, 3)):
        for a in pair:
            bring_own(a).start()

        def start(o):
            for a in pair:
                bring(a, target(o), me).start()

        peers(start)

    edge = jnp.zeros((BLOCK, HEAD_DIM), jnp.bfloat16)
    for ref in (kb, vb):
        ref[0] = edge
        ref[blocks + 1] = edge
    dka[...] = jnp.zeros_like(dka)
    dva[...] = jnp.zeros_like(dva)

    for a in (0, 1):
        bring_own(a).wait()
        peers(lambda o: bring(a, source(o), source(o)).wait_recv())

    def block_step(i):
        for n in range(3):
            at = slice(n * BLOCK, (n + 1) * BLOCK)
            kcat[at] = kb[i + n]
            vcat[at] = vb[i + n]
        gids = [tab_ref[at_gid + i * GLOB + n] for n in range(GLOB)]
        for n in range(GLOB + RAND):
            if n < GLOB:
                named = gids[n]
            else:
                named = tab_ref[at_rid + i * RAND + n - GLOB]
            at = slice((3 + n) * BLOCK, (4 + n) * BLOCK)
            kcat[at] = kb[named + 1]
            vcat[at] = vb[named + 1]
        q = qb[i]
        g = gb[i]
        keys = kcat[...]
        s = dot(keys, q, ((1,), (1,)))
        s = jnp.concatenate(
            [
                jnp.where(i == 0, NEG, s[0:BLOCK]),
                s[BLOCK : 2 * BLOCK],
                jnp.where(i == blocks - 1, NEG, s[2 * BLOCK : 3 * BLOCK]),
                s[3 * BLOCK :],
            ],
            axis=0,
        )
        highest = jnp.max(s, axis=0, keepdims=True)
        e = jnp.exp2((s - highest) * (SCALE * LOG2E))
        p = e * (1.0 / jnp.sum(e, axis=0, keepdims=True))
        dp = dot(vcat[...], g, ((1,), (1,)))
        row_dot = jnp.sum(p * dp, axis=0, keepdims=True)
        ds = (p * (dp - row_dot)).astype(jnp.bfloat16)
        p_low = p.astype(jnp.bfloat16)
        dq = dot(ds, keys, ((0,), (0,))) * SCALE
        dqb[i] = dq.astype(jnp.bfloat16)
        dk = dot(ds, q, ((1,), (0,))) * SCALE
        dv = dot(p_low, g, ((1,), (0,)))
        for n in range(3):
            at = slice(n * BLOCK, (n + 1) * BLOCK)
            dka[i + n] += dk[at]
            dva[i + n] += dv[at]
        for acc, x in ((dka, dk), (dva, dv)):
            for m in range(NGLOB):
                total = acc[m + 1]
                for n in range(GLOB):
                    at = slice((3 + n) * BLOCK, (4 + n) * BLOCK)
                    total += x[at] * wt_ref[((i * GLOB + n) * NGLOB) + m]
                acc[m + 1] = total
        for n in range(RAND):
            at = slice((3 + GLOB + n) * BLOCK, (4 + GLOB + n) * BLOCK)
            terms_k[i * RAND + n] = dk[at].astype(jnp.bfloat16)
            terms_v[i * RAND + n] = dv[at].astype(jnp.bfloat16)

    def attend(o, carry):
        s = source(o)

        @pl.when(o != half)
        def _():
            bring(2, s, s).wait_recv()
            bring(3, s, s).wait_recv()

        @pl.when(o == half)
        def _():
            bring_own(2).wait()
            bring_own(3).wait()

        def inner(b, c):
            block_step(s * each + b)
            return c

        lax.fori_loop(0, each, inner, 0)

        @pl.when(o != half)
        def _():
            give(0, s, me).start()

        @pl.when(o == half)
        def _():
            give_own(0).start()

        return carry

    lax.fori_loop(0, count, attend, 0)

    for a, terms, acc, low in ((1, terms_v, dva, dvb), (2, terms_k, dka, dkb)):

        def scan(e, total):
            total = total * wt_ref[at_carry + e] + terms[tab_ref[at_perm + e]].astype(jnp.float32)
            run[e] = total
            return total

        lax.fori_loop(0, entries, scan, jnp.zeros((BLOCK, HEAD_DIM), jnp.float32))

        def finish(o, carry):
            s = source(o)

            def inner(b, c):
                j = s * each + b
                total = run[tab_ref[at_last + j]] * wt_ref[at_has + j]
                low[j] = (total + acc[j + 1]).astype(jnp.bfloat16)
                return c

            lax.fori_loop(0, each, inner, 0)

            @pl.when(o != half)
            def _():
                give(a, s, me).start()

            @pl.when(o == half)
            def _():
                give_own(a).start()

            return carry

        lax.fori_loop(0, count, finish, 0)

    for a in range(4):
        peers(lambda o: bring(a, target(o), me).wait_send())
    for a in range(3):
        give_own(a).wait()

        def close(o):
            give(a, source(o), me).wait_send()
            give(a, source(o), source(o)).wait_recv()

        peers(close)


def attend_by_head(query, keys, values, grad_out, random_owner, random_within, global_ids):
    count = lax.axis_size("ctx") * lax.axis_size("head")
    tokens, width = query.shape
    rows = tokens * count
    blocks = rows // BLOCK
    entries = blocks * RAND
    low = jnp.bfloat16
    per_owner = blocks // lax.axis_size("ctx")
    named = (random_owner * per_owner + random_within).reshape(-1)
    ids = jnp.arange(entries, dtype=jnp.int32)
    order = named * entries + ids
    rank = jnp.sum((order[None, :] < order[:, None]).astype(jnp.int32), axis=1)
    hit = rank[None, :] == ids[:, None]
    perm = jnp.sum(jnp.where(hit, ids[None, :], 0), axis=1)
    before = jnp.sum((named[None, :] < named[:, None]).astype(jnp.int32), axis=1)
    start = jnp.sum(jnp.where(hit & (before == rank)[None, :], 1, 0), axis=1)
    keys_at = jnp.arange(blocks, dtype=jnp.int32)
    last = jnp.sum((named[None, :] <= keys_at[:, None]).astype(jnp.int32), axis=1) - 1
    has = jnp.any(named[None, :] == keys_at[:, None], axis=1).astype(jnp.int32)
    tab = jnp.concatenate(
        [global_ids.reshape(-1), named, perm, jnp.maximum(last, 0)]
    ).astype(jnp.int32)
    tops = jnp.arange(NGLOB, dtype=jnp.int32)
    picks = (global_ids.reshape(-1)[:, None] == tops).astype(jnp.int32).reshape(-1)
    weights = jnp.concatenate([picks, 1 - start, has]).astype(jnp.float32)
    any_spec = pl.BlockSpec(memory_space=pl.ANY)
    vmem = pltpu.VMEM
    held = lambda n, dtype: vmem((n, BLOCK, HEAD_DIM), dtype)
    in_blocks = lambda x: x.reshape(tokens // BLOCK, BLOCK, width)
    dma = pltpu.SemaphoreType.DMA
    outs = pl.pallas_call(
        head_kernel,
        in_specs=[pl.BlockSpec(memory_space=pltpu.SMEM)] * 2 + [any_spec] * 4,
        out_specs=[any_spec] * 3,
        out_shape=[jax.ShapeDtypeStruct((tokens // BLOCK, BLOCK, width), low)] * 3,
        scratch_shapes=[
            held(blocks + 2, low),
            held(blocks + 2, low),
            held(blocks, low),
            held(blocks, low),
            held(blocks, low),
            held(blocks, low),
            held(blocks, low),
            held(blocks + 2, jnp.float32),
            held(blocks + 2, jnp.float32),
            held(entries, low),
            held(entries, low),
            held(entries, jnp.float32),
            vmem((SLOTS * BLOCK, HEAD_DIM), low),
            vmem((SLOTS * BLOCK, HEAD_DIM), low),
            dma((4, count)),
            dma((4, count)),
            dma((3, count)),
            dma((3, count)),
        ],
        compiler_params=pltpu.CompilerParams(
            collective_id=0, has_side_effects=True, vmem_limit_bytes=VMEM_LIMIT
        ),
        name="head_attention",
    )(tab, weights, *[in_blocks(x) for x in (keys, values, query, grad_out)])
    return tuple(x.reshape(tokens, width) for x in outs)


def on_device(*args):
    devices = lax.axis_size("ctx") * lax.axis_size("head")
    if args[0].shape[1] == devices * HEAD_DIM and devices % 2 == 0:
        return attend_by_head(*args)
    return exchange_and_attend(*args)


def exchange_and_attend(query, keys, values, grad_out, random_owner, random_within, global_ids):
    ctx_count = lax.axis_size("ctx")
    head_count = lax.axis_size("head")
    ctx = lax.axis_index("ctx")
    tokens_in, width_all = query.shape
    features = width_all // head_count
    rows = tokens_in * head_count
    blocks = rows // BLOCK
    half = ctx_count // 2
    place = lax.rem(ctx, half)
    partner = lax.rem(ctx + half, ctx_count)
    flips = jnp.bitwise_xor(place, jnp.arange(half, dtype=jnp.int32))
    swap = [(i, (i + half) % ctx_count) for i in range(ctx_count)]
    up = [(i, i + 1) for i in range(ctx_count - 1)]
    down = [(i + 1, i) for i in range(ctx_count - 1)]
    entries = blocks * RAND
    cap = max(1, (4 * blocks * RAND + 3 * ctx_count - 1) // (3 * ctx_count))

    owner_all = random_owner.reshape(ctx_count, entries)
    within_all = random_within.reshape(ctx_count, entries)
    ids = jnp.arange(entries, dtype=jnp.int32)
    same = owner_all[:, :, None] == owner_all[:, None, :]
    rank_all = jnp.sum(
        jnp.where(same & (ids[None, :] < ids[:, None])[None], 1, 0), axis=2
    ).astype(jnp.int32)
    first = ctx - place
    owner_half = lax.dynamic_slice_in_dim(owner_all, first, half, 0)
    within_rows = lax.dynamic_slice_in_dim(within_all, first, half, 0)
    rank_half = lax.dynamic_slice_in_dim(rank_all, first, half, 0)
    caps = jnp.arange(cap, dtype=jnp.int32)

    def listed(owner):
        hit = (owner_half == owner)[:, :, None] & (rank_half[:, :, None] == caps)
        return jnp.sum(jnp.where(hit, within_rows[:, :, None], 0), axis=1)[flips].reshape(-1)

    own_idx = listed(ctx)
    far_idx = listed(partner)
    owner_mine = lax.dynamic_index_in_dim(owner_all, ctx, 0, keepdims=False)
    rank_mine = lax.dynamic_index_in_dim(rank_all, ctx, 0, keepdims=False)
    far_side = jnp.where(owner_mine // half == ctx // half, 0, 1)
    slots = (jnp.bitwise_xor(owner_mine % half, place) * 2 + far_side) * cap + rank_mine
    gids = lax.dynamic_slice_in_dim(global_ids, ctx * blocks, blocks, 0).reshape(-1)
    edges = jnp.stack([ctx == 0, ctx == ctx_count - 1]).astype(jnp.int32)
    far_flag = (partner == 0).astype(jnp.int32).reshape(1)
    own_flag = (ctx == 0).astype(jnp.int32).reshape(1)
    part = features // CHUNKS

    def to_heads(x, c):
        x = x.reshape(tokens_in, head_count, CHUNKS, part)[:, :, c].reshape(tokens_in, -1)
        return lax.all_to_all(x, "head", split_axis=1, concat_axis=0, tiled=True)

    def to_tokens(parts):
        back = [
            lax.all_to_all(x, "head", split_axis=0, concat_axis=1, tiled=True) for x in parts
        ]
        back = [x.reshape(tokens_in, head_count, part) for x in back]
        return jnp.stack(back, axis=2).reshape(tokens_in, width_all)

    stages = range(CHUNKS)
    kv, kv_far, q, g, incoming = {}, {}, {}, {}, {}
    left, right, summary = {}, {}, {}
    sums, dq, dsum, arrived, firsts, lasts, own, far = {}, {}, {}, {}, {}, {}, {}, {}
    outs = ([], [], [])
    top = NGLOB * BLOCK

    def spread(x):
        found = x
        for d in range(1, half):
            got = lax.ppermute(x, "ctx", [(a * half, a * half + d) for a in range(2)])
            found = jnp.where(place == d, got, found)
        return found

    def collect(x):
        return [
            lax.ppermute(x, "ctx", [(a * half + d, a * half) for a in range(2)])
            for d in range(1, half)
        ]

    def within_half(parts):
        return [parts[0]] + [
            lax.ppermute(
                parts[m],
                "ctx",
                [(i, i // half * half + (i % half ^ m)) for i in range(ctx_count)],
            )
            for m in range(1, half)
        ]

    def fetch(c):
        kv[c] = jnp.stack([to_heads(keys, c), to_heads(values, c)])
        kv_far[c] = lax.ppermute(kv[c], "ctx", swap)
        left[c] = lax.ppermute(kv[c][:, rows - BLOCK :], "ctx", up)
        right[c] = lax.ppermute(kv[c][:, :BLOCK], "ctx", down)
        q[c] = to_heads(query, c)
        g[c] = to_heads(grad_out, c)

    def route(c):
        summary[c] = spread(jnp.where(ctx < half, kv[c][:, :top], kv_far[c][:, :top]))
        ready = (left[c], right[c])
        packed = pack(own_idx, far_idx, kv[c], kv_far[c], ready, half, cap)
        incoming[c] = within_half(packed)

    def attend(c):
        flat = [x.reshape((2 * cap, 2, BLOCK, part)) for x in incoming[c]]
        dq[c], own[c], dleft, dright, dsum[c], *terms = attention(
            gids, slots, edges, q[c], g[c], kv[c], left[c], right[c], summary[c], flat
        )
        sums[c] = [dsum[c]] + collect(dsum[c])
        arrived[c] = within_half([x.reshape((2, cap, 2, BLOCK, part)) for x in terms])
        lasts[c] = lax.ppermute(dleft, "ctx", down)
        firsts[c] = lax.ppermute(dright, "ctx", up)

    def give_back(c):
        col3 = lambda h, *_: (0, 0, h)
        partial_far, dsum[c] = combine(
            far_kernel, 1, jnp.concatenate([far_idx, far_flag]), arrived[c], sums[c], rows,
            [
                pl.BlockSpec((2, rows, HEAD_DIM), col3),
                pl.BlockSpec((2, top, HEAD_DIM), col3),
            ],
            [
                jax.ShapeDtypeStruct((2, rows, part), jnp.bfloat16),
                jax.ShapeDtypeStruct((2, top, part), jnp.float32),
            ],
        )
        far[c] = lax.ppermute(partial_far, "ctx", swap)

    def finish(c):
        tok = pl.BlockSpec((rows, HEAD_DIM), lambda h, *_: (0, h))
        tok_shape = jax.ShapeDtypeStruct((rows, part), jnp.bfloat16)
        dk, dv = combine(
            own_kernel, 0, jnp.concatenate([own_idx, own_flag]), arrived[c],
            (own[c], far[c], firsts[c], lasts[c], dsum[c]),
            rows, [tok, tok], [tok_shape, tok_shape],
        )
        for out, x in zip(outs, (dq[c], dk, dv)):
            out.append(x)

    for step in (fetch, route, attend, give_back, finish):
        for c in stages:
            step(c)
    return tuple(to_tokens(x) for x in outs)


def solution(mesh):
    token = P(("ctx", "head"), None)
    return jax.shard_map(
        on_device,
        mesh=mesh,
        in_specs=(token, token, token, token, P(), P(), P()),
        out_specs=(token, token, token),
        check_vma=False,
    )
```

```python
from functools import partial

import jax
import jax.numpy as jnp
from jax import lax
from jax.experimental import pallas as pl
from jax.experimental.pallas import tpu as pltpu
from jax.sharding import PartitionSpec as P


HEAD_DIM = 128
BLOCK = 128
RAND = 3
GLOB = 2
NGLOB = 4
SLOTS = 3 + GLOB + RAND
CHUNKS = 2
SCALE = HEAD_DIM ** (-0.5)
LOG2E = 1.4426950408889634
NEG = -1e30
VMEM_LIMIT = 60 * 1024 * 1024


def dot(a, b, dims):
    return lax.dot_general(a, b, (dims, ((), ())), preferred_element_type=jnp.float32)


def pack_kernel(own_idx, far_idx, *refs, groups):
    outs = refs[-groups:]
    for m in range(groups):
        outs[m][0, 0] = refs[2 * m][...]
        outs[m][1, 0] = refs[2 * m + 1][...]


def pack(own_idx, far_idx, kv, kv_far, ready, groups, cap):
    features = kv.shape[-1]
    block = (2, BLOCK, features)
    in_specs, args = [], []
    for m in range(groups):
        in_specs.append(pl.BlockSpec(block, lambda c, oi, fi, m=m: (0, oi[m * cap + c], 0)))
        in_specs.append(pl.BlockSpec(block, lambda c, oi, fi, m=m: (0, fi[m * cap + c], 0)))
        args += [kv, kv_far]
    in_specs += [pl.BlockSpec(memory_space=pl.ANY)] * len(ready)
    return pl.pallas_call(
        partial(pack_kernel, groups=groups),
        grid_spec=pltpu.PrefetchScalarGridSpec(
            num_scalar_prefetch=2,
            grid=(cap,),
            in_specs=in_specs,
            out_specs=[
                pl.BlockSpec((2, 1, 2, BLOCK, features), lambda c, *_: (0, c, 0, 0, 0))
            ] * groups,
        ),
        out_shape=[jax.ShapeDtypeStruct((2, cap, 2, BLOCK, features), kv.dtype)] * groups,
        compiler_params=pltpu.CompilerParams(vmem_limit_bytes=VMEM_LIMIT),
        name="pack",
    )(own_idx, far_idx, *args, *ready)


def attn_kernel(
    gid_ref,
    slot_ref,
    edge_ref,
    q_ref,
    g_ref,
    kv_ref,
    left_ref,
    right_ref,
    sum_ref,
    *refs,
    blocks,
    groups,
    each,
):
    incs, refs = refs[:groups], refs[groups:]
    dq_ref, own_ref, dleft_ref, dright_ref, dsum_ref = refs[:5]
    term_outs = refs[5 : 5 + groups]
    kwin, vwin, kcat, vcat, dkw, dvw, sacc, inc_ref, terms_ref = refs[5 + groups :]
    for m in range(groups):
        inc_ref[m * each : (m + 1) * each] = incs[m][...]
    rows = blocks * BLOCK
    for win, x in ((kwin, 0), (vwin, 1)):
        win[0:BLOCK] = left_ref[x]
        win[BLOCK : BLOCK + rows] = kv_ref[x]
        win[BLOCK + rows :] = right_ref[x]
    dkw[...] = jnp.zeros_like(dkw)
    dvw[...] = jnp.zeros_like(dvw)
    sacc[...] = jnp.zeros_like(sacc)
    terms_ref[...] = jnp.zeros_like(terms_ref)

    def step(i, carry):
        base = pl.multiple_of(i * BLOCK, BLOCK)
        here = pl.ds(base, BLOCK)
        window = pl.ds(base, 3 * BLOCK)
        kcat[0 : 3 * BLOCK] = kwin[window]
        vcat[0 : 3 * BLOCK] = vwin[window]
        for n in range(GLOB):
            gid = pl.multiple_of(gid_ref[i * GLOB + n] * BLOCK, BLOCK)
            at = slice((3 + n) * BLOCK, (4 + n) * BLOCK)
            kcat[at] = sum_ref[0, pl.ds(gid, BLOCK)]
            vcat[at] = sum_ref[1, pl.ds(gid, BLOCK)]
        for n in range(RAND):
            slot = slot_ref[i * RAND + n]
            at = slice((3 + GLOB + n) * BLOCK, (4 + GLOB + n) * BLOCK)
            kcat[at] = inc_ref[slot, 0]
            vcat[at] = inc_ref[slot, 1]
        q = q_ref[here]
        g = g_ref[here]
        keys = kcat[...]
        s = dot(keys, q, ((1,), (1,)))
        no_left = (i == 0) & (edge_ref[0] == 1)
        no_right = (i == blocks - 1) & (edge_ref[1] == 1)
        s = jnp.concatenate(
            [
                jnp.where(no_left, NEG, s[0:BLOCK]),
                s[BLOCK : 2 * BLOCK],
                jnp.where(no_right, NEG, s[2 * BLOCK : 3 * BLOCK]),
                s[3 * BLOCK :],
            ],
            axis=0,
        )
        highest = jnp.max(s, axis=0, keepdims=True)
        e = jnp.exp2((s - highest) * (SCALE * LOG2E))
        p = e * (1.0 / jnp.sum(e, axis=0, keepdims=True))
        dp = dot(vcat[...], g, ((1,), (1,)))
        row_dot = jnp.sum(p * dp, axis=0, keepdims=True)
        ds = (p * (dp - row_dot)).astype(jnp.bfloat16)
        p_low = p.astype(jnp.bfloat16)
        dq = dot(ds, keys, ((0,), (0,))) * SCALE
        dq_ref[here] = dq.astype(jnp.bfloat16)
        dk = dot(ds, q, ((1,), (0,))) * SCALE
        dv = dot(p_low, g, ((1,), (0,)))
        dkw[window] += dk[0 : 3 * BLOCK]
        dvw[window] += dv[0 : 3 * BLOCK]
        for n in range(GLOB):
            gid = pl.multiple_of(gid_ref[i * GLOB + n] * BLOCK, BLOCK)
            at = slice((3 + n) * BLOCK, (4 + n) * BLOCK)
            sacc[0, pl.ds(gid, BLOCK)] += dk[at]
            sacc[1, pl.ds(gid, BLOCK)] += dv[at]
        for n in range(RAND):
            slot = slot_ref[i * RAND + n]
            at = slice((3 + GLOB + n) * BLOCK, (4 + GLOB + n) * BLOCK)
            terms_ref[slot, 0] = dk[at].astype(jnp.bfloat16)
            terms_ref[slot, 1] = dv[at].astype(jnp.bfloat16)
        return carry

    lax.fori_loop(0, blocks, step, 0)
    for acc, x in ((dkw, 0), (dvw, 1)):
        dleft_ref[x] = acc[0:BLOCK].astype(jnp.bfloat16)
        own_ref[x] = acc[BLOCK : BLOCK + rows]
        dright_ref[x] = acc[BLOCK + rows :].astype(jnp.bfloat16)
    dsum_ref[...] = sacc[...].astype(jnp.bfloat16)
    for m in range(groups):
        term_outs[m][...] = terms_ref[m * each : (m + 1) * each]


def attention(gids, slots, edges, q, g, kv, left, right, summary, incoming):
    rows, features = q.shape
    blocks = rows // BLOCK
    groups = len(incoming)
    each = incoming[0].shape[0]
    col = lambda h, *_: (0, h)
    col3 = lambda h, *_: (0, 0, h)
    col4 = lambda h, *_: (0, 0, 0, h)
    tok = pl.BlockSpec((rows, HEAD_DIM), col)
    halo = pl.BlockSpec((2, BLOCK, HEAD_DIM), col3)
    summ = pl.BlockSpec((2, NGLOB * BLOCK, HEAD_DIM), col3)
    inc = pl.BlockSpec((each, 2, BLOCK, HEAD_DIM), col4)
    pair = pl.BlockSpec((2, rows, HEAD_DIM), col3)
    low = jnp.bfloat16
    wide = rows + 2 * BLOCK
    return pl.pallas_call(
        partial(attn_kernel, blocks=blocks, groups=groups, each=each),
        grid_spec=pltpu.PrefetchScalarGridSpec(
            num_scalar_prefetch=3,
            grid=(features // HEAD_DIM,),
            in_specs=[tok, tok, pair, halo, halo, summ] + [inc] * groups,
            out_specs=[
                tok,
                pair,
                halo,
                halo,
                summ,
            ]
            + [inc] * groups,
            scratch_shapes=[
                pltpu.VMEM((wide, HEAD_DIM), low),
                pltpu.VMEM((wide, HEAD_DIM), low),
                pltpu.VMEM((SLOTS * BLOCK, HEAD_DIM), low),
                pltpu.VMEM((SLOTS * BLOCK, HEAD_DIM), low),
                pltpu.VMEM((wide, HEAD_DIM), jnp.float32),
                pltpu.VMEM((wide, HEAD_DIM), jnp.float32),
                pltpu.VMEM((2, NGLOB * BLOCK, HEAD_DIM), jnp.float32),
                pltpu.VMEM((groups * each, 2, BLOCK, HEAD_DIM), low),
                pltpu.VMEM((groups * each, 2, BLOCK, HEAD_DIM), low),
            ],
        ),
        out_shape=[
            jax.ShapeDtypeStruct((rows, features), low),
            jax.ShapeDtypeStruct((2, rows, features), jnp.float32),
            jax.ShapeDtypeStruct((2, BLOCK, features), low),
            jax.ShapeDtypeStruct((2, BLOCK, features), low),
            jax.ShapeDtypeStruct((2, NGLOB * BLOCK, features), low),
        ]
        + [jax.ShapeDtypeStruct((each, 2, BLOCK, features), low)] * groups,
        compiler_params=pltpu.CompilerParams(vmem_limit_bytes=VMEM_LIMIT),
        name="attention",
    )(gids, slots, edges, q, g, kv, left, right, summary, *incoming)


def add_slots(acc, idx_ref, incs, cap):
    for m, inc in enumerate(incs):
        for c in range(cap):
            at = pl.ds(pl.multiple_of(idx_ref[m * cap + c] * BLOCK, BLOCK), BLOCK)
            acc[0, at] += inc[0, c, 0].astype(jnp.float32)
            acc[1, at] += inc[0, c, 1].astype(jnp.float32)


def far_kernel(idx_ref, *refs, groups, cap):
    sum_refs = refs[groups : 2 * groups]
    out_ref, total_ref, acc = refs[2 * groups :]
    acc[...] = jnp.zeros_like(acc)
    total = sum_refs[0][...].astype(jnp.float32)
    for ref in sum_refs[1:]:
        total += ref[...].astype(jnp.float32)
    total_ref[...] = total

    @pl.when(idx_ref[groups * cap] == 1)
    def _():
        acc[:, 0 : NGLOB * BLOCK] += total

    add_slots(acc, idx_ref, refs[:groups], cap)
    out_ref[...] = acc[...].astype(jnp.bfloat16)


def own_kernel(idx_ref, *refs, groups, cap):
    own_ref, far_ref, first_ref, last_ref, sum_ref, dk_ref, dv_ref, acc = refs[groups:]
    rows = own_ref.shape[1]
    acc[...] = own_ref[...] + far_ref[...].astype(jnp.float32)
    acc[:, 0:BLOCK] += first_ref[...].astype(jnp.float32)
    acc[:, rows - BLOCK :] += last_ref[...].astype(jnp.float32)

    @pl.when(idx_ref[groups * cap] == 1)
    def _():
        acc[:, 0 : NGLOB * BLOCK] += sum_ref[...]

    add_slots(acc, idx_ref, refs[:groups], cap)
    dk_ref[...] = acc[0].astype(jnp.bfloat16)
    dv_ref[...] = acc[1].astype(jnp.bfloat16)


def combine(kernel, side, idx, incoming, extra, rows, out_specs, out_shape):
    groups = len(incoming)
    cap = incoming[0].shape[1]
    features = incoming[0].shape[-1]
    col3 = lambda h, *_: (0, 0, h)
    spec3 = lambda x: pl.BlockSpec(x.shape[:2] + (HEAD_DIM,), col3)
    inc = pl.BlockSpec((1, cap, 2, BLOCK, HEAD_DIM), lambda h, *_: (side, 0, 0, 0, h))
    return pl.pallas_call(
        partial(kernel, groups=groups, cap=cap),
        grid_spec=pltpu.PrefetchScalarGridSpec(
            num_scalar_prefetch=1,
            grid=(features // HEAD_DIM,),
            in_specs=[inc] * groups + [spec3(x) for x in extra],
            out_specs=out_specs,
            scratch_shapes=[pltpu.VMEM((2, rows, HEAD_DIM), jnp.float32)],
        ),
        out_shape=out_shape,
        compiler_params=pltpu.CompilerParams(vmem_limit_bytes=VMEM_LIMIT),
    )(idx, *incoming, *extra)


def head_kernel(
    tab_ref,
    wt_ref,
    k_in,
    v_in,
    q_in,
    g_in,
    dq_out,
    dk_out,
    dv_out,
    kb,
    vb,
    qb,
    gb,
    dqb,
    dkb,
    dvb,
    dka,
    dva,
    terms_k,
    terms_v,
    run,
    kcat,
    vcat,
    in_send,
    in_recv,
    out_send,
    out_recv,
):
    heads = lax.axis_size("head")
    count = lax.axis_size("ctx") * heads
    half = count // 2
    me = lax.axis_index("ctx") * heads + lax.axis_index("head")
    mine = lax.div(me, half)
    each = k_in.shape[0]
    blocks = count * each
    entries = blocks * RAND
    at_gid, at_rid = 0, blocks * GLOB
    at_perm = at_rid + entries
    at_last = at_perm + entries
    at_carry = blocks * GLOB * NGLOB
    at_has = at_carry + entries

    def side(o):
        return lax.rem(mine + 1 + o, 2) * half

    def target(o):
        return side(o) + lax.rem(me + lax.div(o, 2), half)

    def source(o):
        return side(o) + lax.rem(me + half - lax.div(o, 2), half)

    def coords(t):
        return (lax.div(t, heads), lax.rem(t, heads))

    def rows_of(s):
        return pl.ds(s * each, each)

    def rows_padded(s):
        return pl.ds(s * each + 1, each)

    def cols_of(s):
        return pl.ds(pl.multiple_of(s * HEAD_DIM, HEAD_DIM), HEAD_DIM)

    ins = ((k_in, kb, rows_padded), (v_in, vb, rows_padded), (q_in, qb, rows_of), (g_in, gb, rows_of))
    outs = ((dqb, dq_out), (dvb, dv_out), (dkb, dk_out))

    def bring(a, t, s):
        x, y, rows = ins[a]
        return pltpu.make_async_remote_copy(
            src_ref=x.at[:, :, cols_of(t)],
            dst_ref=y.at[rows(s)],
            send_sem=in_send.at[a, t],
            recv_sem=in_recv.at[a, s],
            device_id=coords(t),
            device_id_type=pl.DeviceIdType.MESH,
        )

    def bring_own(a):
        x, y, rows = ins[a]
        return pltpu.make_async_copy(x.at[:, :, cols_of(me)], y.at[rows(me)], in_recv.at[a, me])

    def give(a, t, s):
        x, y = outs[a]
        return pltpu.make_async_remote_copy(
            src_ref=x.at[rows_of(t)],
            dst_ref=y.at[:, :, cols_of(s)],
            send_sem=out_send.at[a, t],
            recv_sem=out_recv.at[a, s],
            device_id=coords(t),
            device_id_type=pl.DeviceIdType.MESH,
        )

    def give_own(a):
        x, y = outs[a]
        return pltpu.make_async_copy(x.at[rows_of(me)], y.at[:, :, cols_of(me)], out_recv.at[a, me])

    def peers(body):
        def run_body(o, carry):
            body(o)
            return carry

        body(0)
        lax.fori_loop(2, count, run_body, 0)

    barrier = pltpu.get_barrier_semaphore()
    peers(
        lambda o: pl.semaphore_signal(
            barrier, inc=1, device_id=coords(target(o)), device_id_type=pl.DeviceIdType.MESH
        )
    )
    pl.semaphore_wait(barrier, count - 1)

    for pair in ((0, 1), (2, 3)):
        for a in pair:
            bring_own(a).start()

        def start(o):
            for a in pair:
                if a > 1:
                    bring(a - 2, target(o), me).wait_send()
            for a in pair:
                bring(a, target(o), me).start()

        peers(start)

    edge = jnp.zeros((BLOCK, HEAD_DIM), jnp.bfloat16)
    for ref in (kb, vb):
        ref[0] = edge
        ref[blocks + 1] = edge
    dka[...] = jnp.zeros_like(dka)
    dva[...] = jnp.zeros_like(dva)

    for a in (0, 1):
        bring_own(a).wait()
        peers(lambda o: bring(a, source(o), source(o)).wait_recv())

    def block_step(i):
        for n in range(3):
            at = slice(n * BLOCK, (n + 1) * BLOCK)
            kcat[at] = kb[i + n]
            vcat[at] = vb[i + n]
        gids = [tab_ref[at_gid + i * GLOB + n] for n in range(GLOB)]
        for n in range(GLOB + RAND):
            if n < GLOB:
                named = gids[n]
            else:
                named = tab_ref[at_rid + i * RAND + n - GLOB]
            at = slice((3 + n) * BLOCK, (4 + n) * BLOCK)
            kcat[at] = kb[named + 1]
            vcat[at] = vb[named + 1]
        q = qb[i]
        g = gb[i]
        keys = kcat[...]
        s = dot(keys, q, ((1,), (1,)))
        s = jnp.concatenate(
            [
                jnp.where(i == 0, NEG, s[0:BLOCK]),
                s[BLOCK : 2 * BLOCK],
                jnp.where(i == blocks - 1, NEG, s[2 * BLOCK : 3 * BLOCK]),
                s[3 * BLOCK :],
            ],
            axis=0,
        )
        highest = jnp.max(s, axis=0, keepdims=True)
        e = jnp.exp2((s - highest) * (SCALE * LOG2E))
        p = e * (1.0 / jnp.sum(e, axis=0, keepdims=True))
        dp = dot(vcat[...], g, ((1,), (1,)))
        row_dot = jnp.sum(p * dp, axis=0, keepdims=True)
        ds = (p * (dp - row_dot)).astype(jnp.bfloat16)
        p_low = p.astype(jnp.bfloat16)
        dq = dot(ds, keys, ((0,), (0,))) * SCALE
        dqb[i] = dq.astype(jnp.bfloat16)
        dk = dot(ds, q, ((1,), (0,))) * SCALE
        dv = dot(p_low, g, ((1,), (0,)))
        for n in range(3):
            at = slice(n * BLOCK, (n + 1) * BLOCK)
            dka[i + n] += dk[at]
            dva[i + n] += dv[at]
        for acc, x in ((dka, dk), (dva, dv)):
            for m in range(NGLOB):
                total = acc[m + 1]
                for n in range(GLOB):
                    at = slice((3 + n) * BLOCK, (4 + n) * BLOCK)
                    total += x[at] * wt_ref[((i * GLOB + n) * NGLOB) + m]
                acc[m + 1] = total
        for n in range(RAND):
            at = slice((3 + GLOB + n) * BLOCK, (4 + GLOB + n) * BLOCK)
            terms_k[i * RAND + n] = dk[at].astype(jnp.bfloat16)
            terms_v[i * RAND + n] = dv[at].astype(jnp.bfloat16)

    def attend(o, carry):
        s = source(o)

        @pl.when(o != 1)
        def _():
            bring(2, s, s).wait_recv()
            bring(3, s, s).wait_recv()

        @pl.when(o == 1)
        def _():
            bring_own(2).wait()
            bring_own(3).wait()

        def inner(b, c):
            block_step(s * each + b)
            return c

        lax.fori_loop(0, each, inner, 0)

        @pl.when(o != 1)
        def _():
            give(0, s, me).start()

        @pl.when(o == 1)
        def _():
            give_own(0).start()

        return carry

    lax.fori_loop(0, count, attend, 0)

    for a, terms, acc, low in ((1, terms_v, dva, dvb), (2, terms_k, dka, dkb)):

        def scan(e, total):
            total = total * wt_ref[at_carry + e] + terms[tab_ref[at_perm + e]].astype(jnp.float32)
            run[e] = total
            return total

        lax.fori_loop(0, entries, scan, jnp.zeros((BLOCK, HEAD_DIM), jnp.float32))

        def finish(o, carry):
            s = source(o)

            def inner(b, c):
                j = s * each + b
                total = run[tab_ref[at_last + j]] * wt_ref[at_has + j]
                low[j] = (total + acc[j + 1]).astype(jnp.bfloat16)
                return c

            lax.fori_loop(0, each, inner, 0)

            @pl.when(o != 1)
            def _():
                give(a, s, me).start()

            @pl.when(o == 1)
            def _():
                give_own(a).start()

            return carry

        lax.fori_loop(0, count, finish, 0)

    for a in (2, 3):
        peers(lambda o: bring(a, target(o), me).wait_send())
    for a in range(3):
        give_own(a).wait()

        def close(o):
            give(a, source(o), me).wait_send()
            give(a, source(o), source(o)).wait_recv()

        peers(close)


def attend_by_head(query, keys, values, grad_out, random_owner, random_within, global_ids):
    count = lax.axis_size("ctx") * lax.axis_size("head")
    tokens, width = query.shape
    rows = tokens * count
    blocks = rows // BLOCK
    entries = blocks * RAND
    low = jnp.bfloat16
    per_owner = blocks // lax.axis_size("ctx")
    named = (random_owner * per_owner + random_within).reshape(-1)
    ids = jnp.arange(entries, dtype=jnp.int32)
    order = named * entries + ids
    rank = jnp.sum((order[None, :] < order[:, None]).astype(jnp.int32), axis=1)
    hit = rank[None, :] == ids[:, None]
    perm = jnp.sum(jnp.where(hit, ids[None, :], 0), axis=1)
    before = jnp.sum((named[None, :] < named[:, None]).astype(jnp.int32), axis=1)
    start = jnp.sum(jnp.where(hit & (before == rank)[None, :], 1, 0), axis=1)
    keys_at = jnp.arange(blocks, dtype=jnp.int32)
    last = jnp.sum((named[None, :] <= keys_at[:, None]).astype(jnp.int32), axis=1) - 1
    has = jnp.any(named[None, :] == keys_at[:, None], axis=1).astype(jnp.int32)
    tab = jnp.concatenate(
        [global_ids.reshape(-1), named, perm, jnp.maximum(last, 0)]
    ).astype(jnp.int32)
    tops = jnp.arange(NGLOB, dtype=jnp.int32)
    picks = (global_ids.reshape(-1)[:, None] == tops).astype(jnp.int32).reshape(-1)
    weights = jnp.concatenate([picks, 1 - start, has]).astype(jnp.float32)
    any_spec = pl.BlockSpec(memory_space=pl.ANY)
    vmem = pltpu.VMEM
    held = lambda n, dtype: vmem((n, BLOCK, HEAD_DIM), dtype)
    in_blocks = lambda x: x.reshape(tokens // BLOCK, BLOCK, width)
    dma = pltpu.SemaphoreType.DMA
    outs = pl.pallas_call(
        head_kernel,
        in_specs=[pl.BlockSpec(memory_space=pltpu.SMEM)] * 2 + [any_spec] * 4,
        out_specs=[any_spec] * 3,
        out_shape=[jax.ShapeDtypeStruct((tokens // BLOCK, BLOCK, width), low)] * 3,
        scratch_shapes=[
            held(blocks + 2, low),
            held(blocks + 2, low),
            held(blocks, low),
            held(blocks, low),
            held(blocks, low),
            held(blocks, low),
            held(blocks, low),
            held(blocks + 2, jnp.float32),
            held(blocks + 2, jnp.float32),
            held(entries, low),
            held(entries, low),
            held(entries, jnp.float32),
            vmem((SLOTS * BLOCK, HEAD_DIM), low),
            vmem((SLOTS * BLOCK, HEAD_DIM), low),
            dma((4, count)),
            dma((4, count)),
            dma((3, count)),
            dma((3, count)),
        ],
        compiler_params=pltpu.CompilerParams(
            collective_id=0, has_side_effects=True, vmem_limit_bytes=VMEM_LIMIT
        ),
        name="head_attention",
    )(tab, weights, *[in_blocks(x) for x in (keys, values, query, grad_out)])
    return tuple(x.reshape(tokens, width) for x in outs)


def on_device(*args):
    devices = lax.axis_size("ctx") * lax.axis_size("head")
    if args[0].shape[1] == devices * HEAD_DIM and devices % 2 == 0:
        return attend_by_head(*args)
    return exchange_and_attend(*args)


def exchange_and_attend(query, keys, values, grad_out, random_owner, random_within, global_ids):
    ctx_count = lax.axis_size("ctx")
    head_count = lax.axis_size("head")
    ctx = lax.axis_index("ctx")
    tokens_in, width_all = query.shape
    features = width_all // head_count
    rows = tokens_in * head_count
    blocks = rows // BLOCK
    half = ctx_count // 2
    place = lax.rem(ctx, half)
    partner = lax.rem(ctx + half, ctx_count)
    flips = jnp.bitwise_xor(place, jnp.arange(half, dtype=jnp.int32))
    swap = [(i, (i + half) % ctx_count) for i in range(ctx_count)]
    up = [(i, i + 1) for i in range(ctx_count - 1)]
    down = [(i + 1, i) for i in range(ctx_count - 1)]
    entries = blocks * RAND
    cap = max(1, (4 * blocks * RAND + 3 * ctx_count - 1) // (3 * ctx_count))

    owner_all = random_owner.reshape(ctx_count, entries)
    within_all = random_within.reshape(ctx_count, entries)
    ids = jnp.arange(entries, dtype=jnp.int32)
    same = owner_all[:, :, None] == owner_all[:, None, :]
    rank_all = jnp.sum(
        jnp.where(same & (ids[None, :] < ids[:, None])[None], 1, 0), axis=2
    ).astype(jnp.int32)
    first = ctx - place
    owner_half = lax.dynamic_slice_in_dim(owner_all, first, half, 0)
    within_rows = lax.dynamic_slice_in_dim(within_all, first, half, 0)
    rank_half = lax.dynamic_slice_in_dim(rank_all, first, half, 0)
    caps = jnp.arange(cap, dtype=jnp.int32)

    def listed(owner):
        hit = (owner_half == owner)[:, :, None] & (rank_half[:, :, None] == caps)
        return jnp.sum(jnp.where(hit, within_rows[:, :, None], 0), axis=1)[flips].reshape(-1)

    own_idx = listed(ctx)
    far_idx = listed(partner)
    owner_mine = lax.dynamic_index_in_dim(owner_all, ctx, 0, keepdims=False)
    rank_mine = lax.dynamic_index_in_dim(rank_all, ctx, 0, keepdims=False)
    far_side = jnp.where(owner_mine // half == ctx // half, 0, 1)
    slots = (jnp.bitwise_xor(owner_mine % half, place) * 2 + far_side) * cap + rank_mine
    gids = lax.dynamic_slice_in_dim(global_ids, ctx * blocks, blocks, 0).reshape(-1)
    edges = jnp.stack([ctx == 0, ctx == ctx_count - 1]).astype(jnp.int32)
    far_flag = (partner == 0).astype(jnp.int32).reshape(1)
    own_flag = (ctx == 0).astype(jnp.int32).reshape(1)
    part = features // CHUNKS

    def to_heads(x, c):
        x = x.reshape(tokens_in, head_count, CHUNKS, part)[:, :, c].reshape(tokens_in, -1)
        return lax.all_to_all(x, "head", split_axis=1, concat_axis=0, tiled=True)

    def to_tokens(parts):
        back = [
            lax.all_to_all(x, "head", split_axis=0, concat_axis=1, tiled=True) for x in parts
        ]
        back = [x.reshape(tokens_in, head_count, part) for x in back]
        return jnp.stack(back, axis=2).reshape(tokens_in, width_all)

    stages = range(CHUNKS)
    kv, kv_far, q, g, incoming = {}, {}, {}, {}, {}
    left, right, summary = {}, {}, {}
    sums, dq, dsum, arrived, firsts, lasts, own, far = {}, {}, {}, {}, {}, {}, {}, {}
    outs = ([], [], [])
    top = NGLOB * BLOCK

    def spread(x):
        found = x
        for d in range(1, half):
            got = lax.ppermute(x, "ctx", [(a * half, a * half + d) for a in range(2)])
            found = jnp.where(place == d, got, found)
        return found

    def collect(x):
        return [
            lax.ppermute(x, "ctx", [(a * half + d, a * half) for a in range(2)])
            for d in range(1, half)
        ]

    def within_half(parts):
        return [parts[0]] + [
            lax.ppermute(
                parts[m],
                "ctx",
                [(i, i // half * half + (i % half ^ m)) for i in range(ctx_count)],
            )
            for m in range(1, half)
        ]

    def fetch(c):
        kv[c] = jnp.stack([to_heads(keys, c), to_heads(values, c)])
        kv_far[c] = lax.ppermute(kv[c], "ctx", swap)
        left[c] = lax.ppermute(kv[c][:, rows - BLOCK :], "ctx", up)
        right[c] = lax.ppermute(kv[c][:, :BLOCK], "ctx", down)
        q[c] = to_heads(query, c)
        g[c] = to_heads(grad_out, c)

    def route(c):
        summary[c] = spread(jnp.where(ctx < half, kv[c][:, :top], kv_far[c][:, :top]))
        ready = (left[c], right[c])
        packed = pack(own_idx, far_idx, kv[c], kv_far[c], ready, half, cap)
        incoming[c] = within_half(packed)

    def attend(c):
        flat = [x.reshape((2 * cap, 2, BLOCK, part)) for x in incoming[c]]
        dq[c], own[c], dleft, dright, dsum[c], *terms = attention(
            gids, slots, edges, q[c], g[c], kv[c], left[c], right[c], summary[c], flat
        )
        sums[c] = [dsum[c]] + collect(dsum[c])
        arrived[c] = within_half([x.reshape((2, cap, 2, BLOCK, part)) for x in terms])
        lasts[c] = lax.ppermute(dleft, "ctx", down)
        firsts[c] = lax.ppermute(dright, "ctx", up)

    def give_back(c):
        col3 = lambda h, *_: (0, 0, h)
        partial_far, dsum[c] = combine(
            far_kernel, 1, jnp.concatenate([far_idx, far_flag]), arrived[c], sums[c], rows,
            [
                pl.BlockSpec((2, rows, HEAD_DIM), col3),
                pl.BlockSpec((2, top, HEAD_DIM), col3),
            ],
            [
                jax.ShapeDtypeStruct((2, rows, part), jnp.bfloat16),
                jax.ShapeDtypeStruct((2, top, part), jnp.float32),
            ],
        )
        far[c] = lax.ppermute(partial_far, "ctx", swap)

    def finish(c):
        tok = pl.BlockSpec((rows, HEAD_DIM), lambda h, *_: (0, h))
        tok_shape = jax.ShapeDtypeStruct((rows, part), jnp.bfloat16)
        dk, dv = combine(
            own_kernel, 0, jnp.concatenate([own_idx, own_flag]), arrived[c],
            (own[c], far[c], firsts[c], lasts[c], dsum[c]),
            rows, [tok, tok], [tok_shape, tok_shape],
        )
        for out, x in zip(outs, (dq[c], dk, dv)):
            out.append(x)

    for step in (fetch, route, attend, give_back, finish):
        for c in stages:
            step(c)
    return tuple(to_tokens(x) for x in outs)


def solution(mesh):
    token = P(("ctx", "head"), None)
    return jax.shard_map(
        on_device,
        mesh=mesh,
        in_specs=(token, token, token, token, P(), P(), P()),
        out_specs=(token, token, token),
        check_vma=False,
    )
```

```python
from functools import partial

import jax
import jax.numpy as jnp
from jax import lax
from jax.experimental import pallas as pl
from jax.experimental.pallas import tpu as pltpu
from jax.sharding import PartitionSpec as P


HEAD_DIM = 128
BLOCK = 128
RAND = 3
GLOB = 2
NGLOB = 4
SLOTS = 3 + GLOB + RAND
CHUNKS = 2
SCALE = HEAD_DIM ** (-0.5)
LOG2E = 1.4426950408889634
NEG = -1e30
VMEM_LIMIT = 60 * 1024 * 1024


def dot(a, b, dims):
    return lax.dot_general(a, b, (dims, ((), ())), preferred_element_type=jnp.float32)


def pack_kernel(own_idx, far_idx, *refs, groups):
    outs = refs[-groups:]
    for m in range(groups):
        outs[m][0, 0] = refs[2 * m][...]
        outs[m][1, 0] = refs[2 * m + 1][...]


def pack(own_idx, far_idx, kv, kv_far, ready, groups, cap):
    features = kv.shape[-1]
    block = (2, BLOCK, features)
    in_specs, args = [], []
    for m in range(groups):
        in_specs.append(pl.BlockSpec(block, lambda c, oi, fi, m=m: (0, oi[m * cap + c], 0)))
        in_specs.append(pl.BlockSpec(block, lambda c, oi, fi, m=m: (0, fi[m * cap + c], 0)))
        args += [kv, kv_far]
    in_specs += [pl.BlockSpec(memory_space=pl.ANY)] * len(ready)
    return pl.pallas_call(
        partial(pack_kernel, groups=groups),
        grid_spec=pltpu.PrefetchScalarGridSpec(
            num_scalar_prefetch=2,
            grid=(cap,),
            in_specs=in_specs,
            out_specs=[
                pl.BlockSpec((2, 1, 2, BLOCK, features), lambda c, *_: (0, c, 0, 0, 0))
            ] * groups,
        ),
        out_shape=[jax.ShapeDtypeStruct((2, cap, 2, BLOCK, features), kv.dtype)] * groups,
        compiler_params=pltpu.CompilerParams(vmem_limit_bytes=VMEM_LIMIT),
        name="pack",
    )(own_idx, far_idx, *args, *ready)


def attn_kernel(
    gid_ref,
    slot_ref,
    edge_ref,
    q_ref,
    g_ref,
    kv_ref,
    left_ref,
    right_ref,
    sum_ref,
    *refs,
    blocks,
    groups,
    each,
):
    incs, refs = refs[:groups], refs[groups:]
    dq_ref, own_ref, dleft_ref, dright_ref, dsum_ref = refs[:5]
    term_outs = refs[5 : 5 + groups]
    kwin, vwin, kcat, vcat, dkw, dvw, sacc, inc_ref, terms_ref = refs[5 + groups :]
    for m in range(groups):
        inc_ref[m * each : (m + 1) * each] = incs[m][...]
    rows = blocks * BLOCK
    for win, x in ((kwin, 0), (vwin, 1)):
        win[0:BLOCK] = left_ref[x]
        win[BLOCK : BLOCK + rows] = kv_ref[x]
        win[BLOCK + rows :] = right_ref[x]
    dkw[...] = jnp.zeros_like(dkw)
    dvw[...] = jnp.zeros_like(dvw)
    sacc[...] = jnp.zeros_like(sacc)
    terms_ref[...] = jnp.zeros_like(terms_ref)

    def step(i, carry):
        base = pl.multiple_of(i * BLOCK, BLOCK)
        here = pl.ds(base, BLOCK)
        window = pl.ds(base, 3 * BLOCK)
        kcat[0 : 3 * BLOCK] = kwin[window]
        vcat[0 : 3 * BLOCK] = vwin[window]
        for n in range(GLOB):
            gid = pl.multiple_of(gid_ref[i * GLOB + n] * BLOCK, BLOCK)
            at = slice((3 + n) * BLOCK, (4 + n) * BLOCK)
            kcat[at] = sum_ref[0, pl.ds(gid, BLOCK)]
            vcat[at] = sum_ref[1, pl.ds(gid, BLOCK)]
        for n in range(RAND):
            slot = slot_ref[i * RAND + n]
            at = slice((3 + GLOB + n) * BLOCK, (4 + GLOB + n) * BLOCK)
            kcat[at] = inc_ref[slot, 0]
            vcat[at] = inc_ref[slot, 1]
        q = q_ref[here]
        g = g_ref[here]
        keys = kcat[...]
        s = dot(keys, q, ((1,), (1,)))
        no_left = (i == 0) & (edge_ref[0] == 1)
        no_right = (i == blocks - 1) & (edge_ref[1] == 1)
        s = jnp.concatenate(
            [
                jnp.where(no_left, NEG, s[0:BLOCK]),
                s[BLOCK : 2 * BLOCK],
                jnp.where(no_right, NEG, s[2 * BLOCK : 3 * BLOCK]),
                s[3 * BLOCK :],
            ],
            axis=0,
        )
        highest = jnp.max(s, axis=0, keepdims=True)
        e = jnp.exp2((s - highest) * (SCALE * LOG2E))
        p = e * (1.0 / jnp.sum(e, axis=0, keepdims=True))
        dp = dot(vcat[...], g, ((1,), (1,)))
        row_dot = jnp.sum(p * dp, axis=0, keepdims=True)
        ds = (p * (dp - row_dot)).astype(jnp.bfloat16)
        p_low = p.astype(jnp.bfloat16)
        dq = dot(ds, keys, ((0,), (0,))) * SCALE
        dq_ref[here] = dq.astype(jnp.bfloat16)
        dk = dot(ds, q, ((1,), (0,))) * SCALE
        dv = dot(p_low, g, ((1,), (0,)))
        dkw[window] += dk[0 : 3 * BLOCK]
        dvw[window] += dv[0 : 3 * BLOCK]
        for n in range(GLOB):
            gid = pl.multiple_of(gid_ref[i * GLOB + n] * BLOCK, BLOCK)
            at = slice((3 + n) * BLOCK, (4 + n) * BLOCK)
            sacc[0, pl.ds(gid, BLOCK)] += dk[at]
            sacc[1, pl.ds(gid, BLOCK)] += dv[at]
        for n in range(RAND):
            slot = slot_ref[i * RAND + n]
            at = slice((3 + GLOB + n) * BLOCK, (4 + GLOB + n) * BLOCK)
            terms_ref[slot, 0] = dk[at].astype(jnp.bfloat16)
            terms_ref[slot, 1] = dv[at].astype(jnp.bfloat16)
        return carry

    lax.fori_loop(0, blocks, step, 0)
    for acc, x in ((dkw, 0), (dvw, 1)):
        dleft_ref[x] = acc[0:BLOCK].astype(jnp.bfloat16)
        own_ref[x] = acc[BLOCK : BLOCK + rows]
        dright_ref[x] = acc[BLOCK + rows :].astype(jnp.bfloat16)
    dsum_ref[...] = sacc[...].astype(jnp.bfloat16)
    for m in range(groups):
        term_outs[m][...] = terms_ref[m * each : (m + 1) * each]


def attention(gids, slots, edges, q, g, kv, left, right, summary, incoming):
    rows, features = q.shape
    blocks = rows // BLOCK
    groups = len(incoming)
    each = incoming[0].shape[0]
    col = lambda h, *_: (0, h)
    col3 = lambda h, *_: (0, 0, h)
    col4 = lambda h, *_: (0, 0, 0, h)
    tok = pl.BlockSpec((rows, HEAD_DIM), col)
    halo = pl.BlockSpec((2, BLOCK, HEAD_DIM), col3)
    summ = pl.BlockSpec((2, NGLOB * BLOCK, HEAD_DIM), col3)
    inc = pl.BlockSpec((each, 2, BLOCK, HEAD_DIM), col4)
    pair = pl.BlockSpec((2, rows, HEAD_DIM), col3)
    low = jnp.bfloat16
    wide = rows + 2 * BLOCK
    return pl.pallas_call(
        partial(attn_kernel, blocks=blocks, groups=groups, each=each),
        grid_spec=pltpu.PrefetchScalarGridSpec(
            num_scalar_prefetch=3,
            grid=(features // HEAD_DIM,),
            in_specs=[tok, tok, pair, halo, halo, summ] + [inc] * groups,
            out_specs=[
                tok,
                pair,
                halo,
                halo,
                summ,
            ]
            + [inc] * groups,
            scratch_shapes=[
                pltpu.VMEM((wide, HEAD_DIM), low),
                pltpu.VMEM((wide, HEAD_DIM), low),
                pltpu.VMEM((SLOTS * BLOCK, HEAD_DIM), low),
                pltpu.VMEM((SLOTS * BLOCK, HEAD_DIM), low),
                pltpu.VMEM((wide, HEAD_DIM), jnp.float32),
                pltpu.VMEM((wide, HEAD_DIM), jnp.float32),
                pltpu.VMEM((2, NGLOB * BLOCK, HEAD_DIM), jnp.float32),
                pltpu.VMEM((groups * each, 2, BLOCK, HEAD_DIM), low),
                pltpu.VMEM((groups * each, 2, BLOCK, HEAD_DIM), low),
            ],
        ),
        out_shape=[
            jax.ShapeDtypeStruct((rows, features), low),
            jax.ShapeDtypeStruct((2, rows, features), jnp.float32),
            jax.ShapeDtypeStruct((2, BLOCK, features), low),
            jax.ShapeDtypeStruct((2, BLOCK, features), low),
            jax.ShapeDtypeStruct((2, NGLOB * BLOCK, features), low),
        ]
        + [jax.ShapeDtypeStruct((each, 2, BLOCK, features), low)] * groups,
        compiler_params=pltpu.CompilerParams(vmem_limit_bytes=VMEM_LIMIT),
        name="attention",
    )(gids, slots, edges, q, g, kv, left, right, summary, *incoming)


def add_slots(acc, idx_ref, incs, cap):
    for m, inc in enumerate(incs):
        for c in range(cap):
            at = pl.ds(pl.multiple_of(idx_ref[m * cap + c] * BLOCK, BLOCK), BLOCK)
            acc[0, at] += inc[0, c, 0].astype(jnp.float32)
            acc[1, at] += inc[0, c, 1].astype(jnp.float32)


def far_kernel(idx_ref, *refs, groups, cap):
    sum_refs = refs[groups : 2 * groups]
    out_ref, total_ref, acc = refs[2 * groups :]
    acc[...] = jnp.zeros_like(acc)
    total = sum_refs[0][...].astype(jnp.float32)
    for ref in sum_refs[1:]:
        total += ref[...].astype(jnp.float32)
    total_ref[...] = total

    @pl.when(idx_ref[groups * cap] == 1)
    def _():
        acc[:, 0 : NGLOB * BLOCK] += total

    add_slots(acc, idx_ref, refs[:groups], cap)
    out_ref[...] = acc[...].astype(jnp.bfloat16)


def own_kernel(idx_ref, *refs, groups, cap):
    own_ref, far_ref, first_ref, last_ref, sum_ref, dk_ref, dv_ref, acc = refs[groups:]
    rows = own_ref.shape[1]
    acc[...] = own_ref[...] + far_ref[...].astype(jnp.float32)
    acc[:, 0:BLOCK] += first_ref[...].astype(jnp.float32)
    acc[:, rows - BLOCK :] += last_ref[...].astype(jnp.float32)

    @pl.when(idx_ref[groups * cap] == 1)
    def _():
        acc[:, 0 : NGLOB * BLOCK] += sum_ref[...]

    add_slots(acc, idx_ref, refs[:groups], cap)
    dk_ref[...] = acc[0].astype(jnp.bfloat16)
    dv_ref[...] = acc[1].astype(jnp.bfloat16)


def combine(kernel, side, idx, incoming, extra, rows, out_specs, out_shape):
    groups = len(incoming)
    cap = incoming[0].shape[1]
    features = incoming[0].shape[-1]
    col3 = lambda h, *_: (0, 0, h)
    spec3 = lambda x: pl.BlockSpec(x.shape[:2] + (HEAD_DIM,), col3)
    inc = pl.BlockSpec((1, cap, 2, BLOCK, HEAD_DIM), lambda h, *_: (side, 0, 0, 0, h))
    return pl.pallas_call(
        partial(kernel, groups=groups, cap=cap),
        grid_spec=pltpu.PrefetchScalarGridSpec(
            num_scalar_prefetch=1,
            grid=(features // HEAD_DIM,),
            in_specs=[inc] * groups + [spec3(x) for x in extra],
            out_specs=out_specs,
            scratch_shapes=[pltpu.VMEM((2, rows, HEAD_DIM), jnp.float32)],
        ),
        out_shape=out_shape,
        compiler_params=pltpu.CompilerParams(vmem_limit_bytes=VMEM_LIMIT),
    )(idx, *incoming, *extra)


HEAD_VMEM = 48 * 1024 * 1024


def store_kernel(*refs):
    sems = refs[6]
    copies = [pltpu.make_async_copy(refs[m], refs[3 + m], sems.at[m]) for m in range(3)]
    for copy in copies:
        copy.start()
    for copy in copies:
        copy.wait()


def head_kernel(
    owner_ref,
    within_ref,
    global_ref,
    owner_vec,
    within_vec,
    k_in,
    v_in,
    q_in,
    g_in,
    dq_out,
    dk_out,
    dv_out,
    kb,
    vb,
    qb,
    gb,
    dqb,
    dka,
    dva,
    terms_k,
    terms_v,
    run,
    kcat,
    vcat,
    sorted_ref,
    last_ref,
    has_ref,
    in_send,
    in_recv,
    out_send,
    out_recv,
):
    heads = lax.axis_size("head")
    count = lax.axis_size("ctx") * heads
    half = count // 2
    me = lax.axis_index("ctx") * heads + lax.axis_index("head")
    mine = lax.div(me, half)
    each = k_in.shape[0]
    blocks = count * each
    entries = blocks * RAND
    per_owner = lax.div(blocks, lax.axis_size("ctx"))

    def named_of(i, r):
        return owner_ref[r, i] * per_owner + within_ref[r, i]

    def same(a, b):
        return (1 - jnp.minimum(jnp.abs(a - b), 1)).astype(jnp.float32)

    def side(o):
        return lax.rem(mine + 1 + o, 2) * half

    def target(o):
        return side(o) + lax.rem(me + lax.div(o, 2), half)

    def source(o):
        return side(o) + lax.rem(me + half - lax.div(o, 2), half)

    def coords(t):
        return (lax.div(t, heads), lax.rem(t, heads))

    def rows_of(s):
        return pl.ds(s * each, each)

    def rows_padded(s):
        return pl.ds(s * each + 1, each)

    def cols_of(s):
        return pl.ds(pl.multiple_of(s * HEAD_DIM, HEAD_DIM), HEAD_DIM)

    ins = ((k_in, kb, rows_padded), (v_in, vb, rows_padded), (q_in, qb, rows_of), (g_in, gb, rows_of))
    outs = ((dqb, dq_out), (qb, dv_out), (gb, dk_out))

    def bring(a, t, s):
        x, y, rows = ins[a]
        return pltpu.make_async_remote_copy(
            src_ref=x.at[:, :, cols_of(t)],
            dst_ref=y.at[rows(s)],
            send_sem=in_send.at[a, t],
            recv_sem=in_recv.at[a, s],
            device_id=coords(t),
            device_id_type=pl.DeviceIdType.MESH,
        )

    def bring_own(a):
        x, y, rows = ins[a]
        return pltpu.make_async_copy(x.at[:, :, cols_of(me)], y.at[rows(me)], in_recv.at[a, me])

    def give(a, t, s):
        x, y = outs[a]
        return pltpu.make_async_remote_copy(
            src_ref=x.at[rows_of(t)],
            dst_ref=y.at[:, :, cols_of(s)],
            send_sem=out_send.at[a, t],
            recv_sem=out_recv.at[a, s],
            device_id=coords(t),
            device_id_type=pl.DeviceIdType.MESH,
        )

    def give_own(a):
        x, y = outs[a]
        return pltpu.make_async_copy(x.at[rows_of(me)], y.at[:, :, cols_of(me)], out_recv.at[a, me])

    def peers(body):
        def run_body(o, carry):
            body(o)
            return carry

        body(0)
        lax.fori_loop(2, count, run_body, 0)

    barrier = pltpu.get_barrier_semaphore()
    peers(
        lambda o: pl.semaphore_signal(
            barrier, inc=1, device_id=coords(target(o)), device_id_type=pl.DeviceIdType.MESH
        )
    )
    pl.semaphore_wait(barrier, count - 1)

    def build_lists():
        named = owner_vec[...] * per_owner + within_vec[...]
        place = lax.broadcasted_iota(jnp.int32, named.shape, 0) * blocks
        place += lax.broadcasted_iota(jnp.int32, named.shape, 1)
        order = named * entries + place
        rank = jnp.zeros_like(order)
        for r in range(RAND):

            def count_below(i, rank):
                mark = named_of(i, r) * entries + r * blocks + i
                return rank + jnp.minimum(jnp.maximum(order - mark, 0), 1)

            rank = lax.fori_loop(0, blocks, count_below, rank)

        def sort_step(e, carry):
            sorted_ref[e] = jnp.sum(jnp.where(rank == e, order, 0))
            return carry

        lax.fori_loop(0, entries, sort_step, 0)

        def span_step(j, carry):
            upto = jnp.sum(jnp.where(named <= j, 1, 0))
            last_ref[j] = jnp.maximum(upto - 1, 0)
            has_ref[j] = jnp.minimum(jnp.sum(jnp.where(named == j, 1, 0)), 1)
            return carry

        lax.fori_loop(0, blocks, span_step, 0)

    for pair in ((0, 1), (2, 3)):
        if pair == (2, 3):
            build_lists()
        for a in pair:
            bring_own(a).start()

        def start(o):
            for a in pair:
                if a > 1:
                    bring(a - 2, target(o), me).wait_send()
            for a in pair:
                bring(a, target(o), me).start()

        peers(start)

    edge = jnp.zeros((BLOCK, HEAD_DIM), jnp.bfloat16)
    for ref in (kb, vb):
        ref[0] = edge
        ref[blocks + 1] = edge
    dka[...] = jnp.zeros_like(dka)
    dva[...] = jnp.zeros_like(dva)

    for a in (0, 1):
        bring_own(a).wait()
        peers(lambda o: bring(a, source(o), source(o)).wait_recv())

    def block_step(i):
        for n in range(3):
            at = slice(n * BLOCK, (n + 1) * BLOCK)
            kcat[at] = kb[i + n]
            vcat[at] = vb[i + n]
        gids = [global_ref[n, i] for n in range(GLOB)]
        for n in range(GLOB + RAND):
            if n < GLOB:
                named = gids[n]
            else:
                named = named_of(i, n - GLOB)
            at = slice((3 + n) * BLOCK, (4 + n) * BLOCK)
            kcat[at] = kb[named + 1]
            vcat[at] = vb[named + 1]
        q = qb[i]
        g = gb[i]
        keys = kcat[...]
        s = dot(keys, q, ((1,), (1,)))
        s = jnp.concatenate(
            [
                jnp.where(i == 0, NEG, s[0:BLOCK]),
                s[BLOCK : 2 * BLOCK],
                jnp.where(i == blocks - 1, NEG, s[2 * BLOCK : 3 * BLOCK]),
                s[3 * BLOCK :],
            ],
            axis=0,
        )
        highest = jnp.max(s, axis=0, keepdims=True)
        e = jnp.exp2((s - highest) * (SCALE * LOG2E))
        p = e * (1.0 / jnp.sum(e, axis=0, keepdims=True))
        dp = dot(vcat[...], g, ((1,), (1,)))
        row_dot = jnp.sum(p * dp, axis=0, keepdims=True)
        ds = (p * (dp - row_dot)).astype(jnp.bfloat16)
        p_low = p.astype(jnp.bfloat16)
        dq = dot(ds, keys, ((0,), (0,))) * SCALE
        dqb[i] = dq.astype(jnp.bfloat16)
        dk = dot(ds, q, ((1,), (0,))) * SCALE
        dv = dot(p_low, g, ((1,), (0,)))
        for n in range(3):
            at = slice(n * BLOCK, (n + 1) * BLOCK)
            dka[i + n] += dk[at]
            dva[i + n] += dv[at]
        for acc, x in ((dka, dk), (dva, dv)):
            for m in range(NGLOB):
                total = acc[m + 1]
                for n in range(GLOB):
                    at = slice((3 + n) * BLOCK, (4 + n) * BLOCK)
                    total += x[at] * same(gids[n], m)
                acc[m + 1] = total
        for n in range(RAND):
            at = slice((3 + GLOB + n) * BLOCK, (4 + GLOB + n) * BLOCK)
            terms_k[n * blocks + i] = dk[at].astype(jnp.bfloat16)
            terms_v[n * blocks + i] = dv[at].astype(jnp.bfloat16)

    def attend(o, carry):
        s = source(o)

        @pl.when(o != 1)
        def _():
            bring(2, s, s).wait_recv()
            bring(3, s, s).wait_recv()

        @pl.when(o == 1)
        def _():
            bring_own(2).wait()
            bring_own(3).wait()

        def inner(b, c):
            block_step(s * each + b)
            return c

        lax.fori_loop(0, each, inner, 0)

        @pl.when(o != 1)
        def _():
            give(0, s, me).start()

        @pl.when(o == 1)
        def _():
            give_own(0).start()

        return carry

    lax.fori_loop(0, count, attend, 0)

    for a, terms, acc, low in ((1, terms_v, dva, qb), (2, terms_k, dka, gb)):

        def scan(e, carry):
            total, before = carry
            block = lax.div(sorted_ref[e], entries)
            term = terms[lax.rem(sorted_ref[e], entries)].astype(jnp.float32)
            total = total * same(block, before) + term
            run[e] = total
            return total, block

        none = jnp.zeros((BLOCK, HEAD_DIM), jnp.float32)
        lax.fori_loop(0, entries, scan, (none, jnp.int32(0)))

        def finish(o, carry):
            s = source(o)

            def inner(b, c):
                j = s * each + b
                total = run[last_ref[j]] * has_ref[j].astype(jnp.float32)
                low[j] = (total + acc[j + 1]).astype(jnp.bfloat16)
                return c

            lax.fori_loop(0, each, inner, 0)

            @pl.when(o != 1)
            def _():
                give(a, s, me).start()

            @pl.when(o == 1)
            def _():
                give_own(a).start()

            return carry

        lax.fori_loop(0, count, finish, 0)

    for a in (2, 3):
        peers(lambda o: bring(a, target(o), me).wait_send())
    for a in range(3):
        give_own(a).wait()

        def close(o):
            give(a, source(o), me).wait_send()
            give(a, source(o), source(o)).wait_recv()

        peers(close)


def attend_by_head(query, keys, values, grad_out, random_owner, random_within, global_ids):
    count = lax.axis_size("ctx") * lax.axis_size("head")
    tokens, width = query.shape
    rows = tokens * count
    blocks = rows // BLOCK
    entries = blocks * RAND
    low = jnp.bfloat16
    any_spec = pl.BlockSpec(memory_space=pl.ANY)
    smem_spec = pl.BlockSpec(memory_space=pltpu.SMEM)
    vmem_spec = pl.BlockSpec(memory_space=pltpu.VMEM)
    owner, within, named = random_owner.T, random_within.T, global_ids.T
    vmem = pltpu.VMEM
    held = lambda n, dtype: vmem((n, BLOCK, HEAD_DIM), dtype)
    in_blocks = lambda x: x.reshape(tokens // BLOCK, BLOCK, width)
    dma = pltpu.SemaphoreType.DMA
    outs = pl.pallas_call(
        head_kernel,
        in_specs=[smem_spec] * 3 + [vmem_spec] * 2 + [any_spec] * 4,
        out_specs=[vmem_spec] * 3,
        out_shape=[vmem((tokens // BLOCK, BLOCK, width), low)] * 3,
        scratch_shapes=[
            held(blocks + 2, low),
            held(blocks + 2, low),
            held(blocks, low),
            held(blocks, low),
            held(blocks, low),
            held(blocks + 2, jnp.float32),
            held(blocks + 2, jnp.float32),
            held(entries, low),
            held(entries, low),
            held(entries, jnp.float32),
            vmem((SLOTS * BLOCK, HEAD_DIM), low),
            vmem((SLOTS * BLOCK, HEAD_DIM), low),
            pltpu.SMEM((entries,), jnp.int32),
            pltpu.SMEM((blocks,), jnp.int32),
            pltpu.SMEM((blocks,), jnp.int32),
            dma((4, count)),
            dma((4, count)),
            dma((3, count)),
            dma((3, count)),
        ],
        compiler_params=pltpu.CompilerParams(
            collective_id=0, has_side_effects=True, vmem_limit_bytes=HEAD_VMEM
        ),
        name="head_attention",
    )(owner, within, named, owner, within, *[in_blocks(x) for x in (keys, values, query, grad_out)])
    outs = pl.pallas_call(
        store_kernel,
        in_specs=[vmem_spec] * 3,
        out_specs=[any_spec] * 3,
        out_shape=[jax.ShapeDtypeStruct((tokens // BLOCK, BLOCK, width), low)] * 3,
        scratch_shapes=[dma((3,))],
        compiler_params=pltpu.CompilerParams(vmem_limit_bytes=2 * 1024 * 1024),
        name="store",
    )(*outs)
    return tuple(x.reshape(tokens, width) for x in outs)


def on_device(*args):
    devices = lax.axis_size("ctx") * lax.axis_size("head")
    if args[0].shape[1] == devices * HEAD_DIM and devices % 2 == 0:
        return attend_by_head(*args)
    return exchange_and_attend(*args)


def exchange_and_attend(query, keys, values, grad_out, random_owner, random_within, global_ids):
    ctx_count = lax.axis_size("ctx")
    head_count = lax.axis_size("head")
    ctx = lax.axis_index("ctx")
    tokens_in, width_all = query.shape
    features = width_all // head_count
    rows = tokens_in * head_count
    blocks = rows // BLOCK
    half = ctx_count // 2
    place = lax.rem(ctx, half)
    partner = lax.rem(ctx + half, ctx_count)
    flips = jnp.bitwise_xor(place, jnp.arange(half, dtype=jnp.int32))
    swap = [(i, (i + half) % ctx_count) for i in range(ctx_count)]
    up = [(i, i + 1) for i in range(ctx_count - 1)]
    down = [(i + 1, i) for i in range(ctx_count - 1)]
    entries = blocks * RAND
    cap = max(1, (4 * blocks * RAND + 3 * ctx_count - 1) // (3 * ctx_count))

    owner_all = random_owner.reshape(ctx_count, entries)
    within_all = random_within.reshape(ctx_count, entries)
    ids = jnp.arange(entries, dtype=jnp.int32)
    same = owner_all[:, :, None] == owner_all[:, None, :]
    rank_all = jnp.sum(
        jnp.where(same & (ids[None, :] < ids[:, None])[None], 1, 0), axis=2
    ).astype(jnp.int32)
    first = ctx - place
    owner_half = lax.dynamic_slice_in_dim(owner_all, first, half, 0)
    within_rows = lax.dynamic_slice_in_dim(within_all, first, half, 0)
    rank_half = lax.dynamic_slice_in_dim(rank_all, first, half, 0)
    caps = jnp.arange(cap, dtype=jnp.int32)

    def listed(owner):
        hit = (owner_half == owner)[:, :, None] & (rank_half[:, :, None] == caps)
        return jnp.sum(jnp.where(hit, within_rows[:, :, None], 0), axis=1)[flips].reshape(-1)

    own_idx = listed(ctx)
    far_idx = listed(partner)
    owner_mine = lax.dynamic_index_in_dim(owner_all, ctx, 0, keepdims=False)
    rank_mine = lax.dynamic_index_in_dim(rank_all, ctx, 0, keepdims=False)
    far_side = jnp.where(owner_mine // half == ctx // half, 0, 1)
    slots = (jnp.bitwise_xor(owner_mine % half, place) * 2 + far_side) * cap + rank_mine
    gids = lax.dynamic_slice_in_dim(global_ids, ctx * blocks, blocks, 0).reshape(-1)
    edges = jnp.stack([ctx == 0, ctx == ctx_count - 1]).astype(jnp.int32)
    far_flag = (partner == 0).astype(jnp.int32).reshape(1)
    own_flag = (ctx == 0).astype(jnp.int32).reshape(1)
    part = features // CHUNKS

    def to_heads(x, c):
        x = x.reshape(tokens_in, head_count, CHUNKS, part)[:, :, c].reshape(tokens_in, -1)
        return lax.all_to_all(x, "head", split_axis=1, concat_axis=0, tiled=True)

    def to_tokens(parts):
        back = [
            lax.all_to_all(x, "head", split_axis=0, concat_axis=1, tiled=True) for x in parts
        ]
        back = [x.reshape(tokens_in, head_count, part) for x in back]
        return jnp.stack(back, axis=2).reshape(tokens_in, width_all)

    stages = range(CHUNKS)
    kv, kv_far, q, g, incoming = {}, {}, {}, {}, {}
    left, right, summary = {}, {}, {}
    sums, dq, dsum, arrived, firsts, lasts, own, far = {}, {}, {}, {}, {}, {}, {}, {}
    outs = ([], [], [])
    top = NGLOB * BLOCK

    def spread(x):
        found = x
        for d in range(1, half):
            got = lax.ppermute(x, "ctx", [(a * half, a * half + d) for a in range(2)])
            found = jnp.where(place == d, got, found)
        return found

    def collect(x):
        return [
            lax.ppermute(x, "ctx", [(a * half + d, a * half) for a in range(2)])
            for d in range(1, half)
        ]

    def within_half(parts):
        return [parts[0]] + [
            lax.ppermute(
                parts[m],
                "ctx",
                [(i, i // half * half + (i % half ^ m)) for i in range(ctx_count)],
            )
            for m in range(1, half)
        ]

    def fetch(c):
        kv[c] = jnp.stack([to_heads(keys, c), to_heads(values, c)])
        kv_far[c] = lax.ppermute(kv[c], "ctx", swap)
        left[c] = lax.ppermute(kv[c][:, rows - BLOCK :], "ctx", up)
        right[c] = lax.ppermute(kv[c][:, :BLOCK], "ctx", down)
        q[c] = to_heads(query, c)
        g[c] = to_heads(grad_out, c)

    def route(c):
        summary[c] = spread(jnp.where(ctx < half, kv[c][:, :top], kv_far[c][:, :top]))
        ready = (left[c], right[c])
        packed = pack(own_idx, far_idx, kv[c], kv_far[c], ready, half, cap)
        incoming[c] = within_half(packed)

    def attend(c):
        flat = [x.reshape((2 * cap, 2, BLOCK, part)) for x in incoming[c]]
        dq[c], own[c], dleft, dright, dsum[c], *terms = attention(
            gids, slots, edges, q[c], g[c], kv[c], left[c], right[c], summary[c], flat
        )
        sums[c] = [dsum[c]] + collect(dsum[c])
        arrived[c] = within_half([x.reshape((2, cap, 2, BLOCK, part)) for x in terms])
        lasts[c] = lax.ppermute(dleft, "ctx", down)
        firsts[c] = lax.ppermute(dright, "ctx", up)

    def give_back(c):
        col3 = lambda h, *_: (0, 0, h)
        partial_far, dsum[c] = combine(
            far_kernel, 1, jnp.concatenate([far_idx, far_flag]), arrived[c], sums[c], rows,
            [
                pl.BlockSpec((2, rows, HEAD_DIM), col3),
                pl.BlockSpec((2, top, HEAD_DIM), col3),
            ],
            [
                jax.ShapeDtypeStruct((2, rows, part), jnp.bfloat16),
                jax.ShapeDtypeStruct((2, top, part), jnp.float32),
            ],
        )
        far[c] = lax.ppermute(partial_far, "ctx", swap)

    def finish(c):
        tok = pl.BlockSpec((rows, HEAD_DIM), lambda h, *_: (0, h))
        tok_shape = jax.ShapeDtypeStruct((rows, part), jnp.bfloat16)
        dk, dv = combine(
            own_kernel, 0, jnp.concatenate([own_idx, own_flag]), arrived[c],
            (own[c], far[c], firsts[c], lasts[c], dsum[c]),
            rows, [tok, tok], [tok_shape, tok_shape],
        )
        for out, x in zip(outs, (dq[c], dk, dv)):
            out.append(x)

    for step in (fetch, route, attend, give_back, finish):
        for c in stages:
            step(c)
    return tuple(to_tokens(x) for x in outs)


def solution(mesh):
    token = P(("ctx", "head"), None)
    return jax.shard_map(
        on_device,
        mesh=mesh,
        in_specs=(token, token, token, token, P(), P(), P()),
        out_specs=(token, token, token),
        check_vma=False,
    )
```
